32 devices in a mesh: seq: 8 (over z, y), head: 4 (over x, core).
Axes of the slice: x: 2, y: 2, z: 4, core: 2. Of those that a mesh axis runs over, the one named last changes fastest.
Arguments:
- tokens: bfloat16 [16384, 1024], P(('seq', 'head')), may hold values from -6 to 6
- mod_shift: float32 [1024], replicated, may hold values from -3 to 3
- mod_scale: float32 [1024], replicated, may hold values from -3 to 3
- attn_gate: float32 [1024], replicated, may hold values from -4 to 4
- w_qkv: bfloat16 [1024, 3072], replicated, may hold values from -0.1875 to 0.1875
- query_gain: float32 [1024], replicated, may hold values from 0.5 to 8
- key_gain: float32 [1024], replicated, may hold values from 0.5 to 8
- w_out: bfloat16 [1024, 1024], replicated, may hold values from -0.1875 to 0.1875
- w_dec: bfloat16 [1024, 128], replicated, may hold values from -0.1875 to 0.1875
- conv_weight: bfloat16 [3456, 128], replicated, may hold values from -0.109375 to 0.109375
- block_lists: int32 [256, 8], P('seq'), may hold values from 0 to 255, as said below
- active_blocks: int32 [32], replicated, may hold values from 4 to 8
- to_next: int32 [4096], P(('seq', 'head')), may hold values from 0 to 511
- to_prev: int32 [4096], P(('seq', 'head')), may hold values from 0 to 511
- conv_table: int32 [16384, 27], P(('seq', 'head')), may hold values from 0 to 768
Outputs:
- block_out: bfloat16 [16384, 1024], P(('seq', 'head'))
- decoded: bfloat16 [16384, 128], P(('seq', 'head'))
The draws below stay inside these ranges and needn't reach their ends.
Inputs may be any that keep to these rules, and one draw needn't show every extreme that they name: `block_lists`: row g names block g first; all its entries lie within 16 blocks of the range of 32 blocks holding g: from max(0, (g // 32) * 32 - 16) to min(256, (g // 32 + 1) * 32 + 16) - 1, and both ends are named in every range that has them.
All inputs are finite; a program needn't handle non-finite values.
Results may differ from the reference program's by a relative error of at most 0.007.
The reference program's roundings to bfloat16 on the way (of `normed`, `weights`, `attended`, `features` and `buffer`) count: a program that leaves them out, or rounds other values in their place, can miss the bound.
Values may be sent and summed in bfloat16 or wider, within the bound.
A program may use at most 128 MiB of HBM per device.

```python
import math
import jax
import jax.numpy as jnp
from jax import lax

D = 1024
HEADS = 16
HD = 64
C = 128
BLK = 64
KB = 8
TAPS = 27
TOK_DEV = 512
NB_DEV = 8
GB = 32
HB = 16
FACE = 128
TOKENS = 16384
NBLOCKS = 256
N_SEQ = 8
DEVICES = 32


def draw_query_gain(key, part):
    folded = jax.random.fold_in(key, 11)
    lowest, highest = (math.log(0.5), math.log(2.0))
    return jnp.exp(jax.random.uniform(folded, (D,), jnp.float32, lowest, highest))


def draw_key_gain(key, part):
    folded = jax.random.fold_in(key, 12)
    lowest, highest = (math.log(0.5), math.log(2.0))
    return jnp.exp(jax.random.uniform(folded, (D,), jnp.float32, lowest, highest))


def draw_block_lists(key, part):
    folded = jax.random.fold_in(key, 21)
    block_ids = jnp.arange(NBLOCKS, dtype=jnp.int32)
    ranges = block_ids // GB
    lowest = jnp.maximum(ranges * GB - HB, 0)
    highest = jnp.minimum((ranges + 1) * GB + HB, NBLOCKS)
    raw_picks = jax.random.randint(folded, (NBLOCKS, KB - 1), 0, 1 << 20, dtype=jnp.int32)
    picks = lowest[:, None] + raw_picks % (highest - lowest)[:, None]
    inside = block_ids % GB
    first_pick = jnp.where(inside == 0, lowest, jnp.where(inside == GB - 1, highest - 1, picks[:, 0]))
    picks = picks.at[:, 0].set(first_pick)
    return jnp.concatenate([block_ids[:, None], picks], axis=1).astype(jnp.int32)


def place_ends(array, own_key, smallest, top_value):
    longest = array.shape.index(max(array.shape))
    spots = []
    for shift in (0, 1):
        where = [jax.random.randint(jax.random.fold_in(own_key, axis), (), 0, length) for axis, length in enumerate(array.shape)]
        where[longest] = (where[longest] + shift) % array.shape[longest]
        spots.append(tuple(where))
    return array.at[spots[0]].set(smallest).at[spots[1]].set(top_value)


def steps_of(own_key, shape, pieces, smallest, largest):
    loudness = 1.0
    for dim, parts in pieces:
        steps = jax.random.uniform(jax.random.fold_in(jax.random.fold_in(own_key, 6), dim), (parts,), jnp.float32, smallest / len(pieces), largest / len(pieces))
        loudness = loudness * jnp.repeat(jnp.exp(steps), shape[dim] // parts).reshape((-1,) + (1,) * (len(shape) - 1 - dim))
    return loudness


def scatter_about(own_key, extent, width, bound, shards=(), held_as=jnp.bfloat16):
    result = jax.random.normal(own_key, extent, jnp.float32) * width
    if len(shards) > 0:
        result = steps_of(own_key, extent, shards, -0.22, 0.18) * result
    return jnp.clip(result, min=-bound, max=bound).astype(held_as)


def setup_inputs(seed: int = 0) -> dict:
    key_list = jax.random.split(jax.random.key(seed), 16)
    return {
        "tokens": scatter_about(key_list[0], (TOKENS, D), 1.0, 6.0, ((0, 32),)),
        "mod_shift": scatter_about(key_list[1], (D,), 0.5, 3.0, (), jnp.float32),
        "mod_scale": scatter_about(key_list[2], (D,), 0.5, 3.0, (), jnp.float32),
        "attn_gate": scatter_about(key_list[3], (D,), 1.0, 4.0, (), jnp.float32),
        "w_qkv": scatter_about(key_list[4], (D, 3 * D), D ** -0.5, 0.1875),
        "query_gain": draw_query_gain(jax.random.fold_in(key_list[15], 71), 0),
        "key_gain": draw_key_gain(jax.random.fold_in(key_list[15], 71), 0),
        "w_out": scatter_about(key_list[7], (D, D), D ** -0.5, 0.1875),
        "w_dec": scatter_about(key_list[8], (D, C), D ** -0.5, 0.1875),
        "conv_weight": scatter_about(key_list[9], (TAPS * C, C), (TAPS * C) ** -0.5, 0.109375),
        "block_lists": draw_block_lists(jax.random.fold_in(key_list[15], 71), 0),
        "active_blocks": place_ends(jax.random.randint(key_list[11], (DEVICES,), (NB_DEV + 1) // 2, NB_DEV + 1), jax.random.fold_in(key_list[11], 1), (NB_DEV + 1) // 2, NB_DEV).astype(jnp.int32),
        "to_next": place_ends(jax.random.randint(key_list[12], (DEVICES * FACE,), 0, TOK_DEV), jax.random.fold_in(key_list[12], 1), 0, TOK_DEV - 1).astype(jnp.int32),
        "to_prev": place_ends(jax.random.randint(key_list[13], (DEVICES * FACE,), 0, TOK_DEV), jax.random.fold_in(key_list[13], 1), 0, TOK_DEV - 1).astype(jnp.int32),
        "conv_table": place_ends(jax.random.randint(key_list[14], (TOKENS, TAPS), 0, TOK_DEV + 2 * FACE + 1), jax.random.fold_in(key_list[14], 1), 0, TOK_DEV + 2 * FACE).astype(jnp.int32),
    }


EPSILON = 1e-06
MASKED = -1000000000.0

def layer_norm(values, mod_shift, mod_scale):
    centre = lax.optimization_barrier(jnp.mean(values, axis=-1, keepdims=True))
    centred = values - centre
    spread = lax.optimization_barrier(jnp.mean(centred * centred, axis=-1, keepdims=True))
    return centred * lax.rsqrt(spread + EPSILON) * (1.0 + mod_scale) + mod_shift

def head_norm(values, gain_row):
    per_head = values.reshape(values.shape[0], -1, HD)
    scaling = lax.rsqrt(lax.optimization_barrier(jnp.mean(per_head * per_head, axis=-1, keepdims=True)) + EPSILON)
    return (per_head * scaling).reshape(values.shape) * gain_row

def project(token_rows, mod_shift, mod_scale, w_qkv, query_gain, key_gain):
    normed = layer_norm(token_rows.astype(jnp.float32), mod_shift, mod_scale).astype(jnp.bfloat16)
    projected = jnp.dot(normed, w_qkv, preferred_element_type=jnp.float32)
    queries = head_norm(projected[:, :D], query_gain).astype(jnp.bfloat16)
    key_part = head_norm(projected[:, D:2 * D], key_gain).astype(jnp.bfloat16)
    values = projected[:, 2 * D:].astype(jnp.bfloat16)
    return (queries, key_part, values)

def block_flags(block_ids, active_blocks):
    owners = block_ids // NB_DEV
    slot_index = block_ids % NB_DEV
    owner_ids = jnp.arange(active_blocks.shape[0], dtype=jnp.int32)
    counted = lax.optimization_barrier(jnp.sum(jnp.where(owners[..., None] == owner_ids, active_blocks, 0), axis=-1))
    return slot_index < counted

def attend(queries, key_rows, value_rows, live_keys):
    scores = jnp.einsum('bqhd,bkhd->bhqk', queries.astype(jnp.float32), key_rows.astype(jnp.float32)) * (1.0 / math.sqrt(HD))
    penalty = jnp.where(jnp.repeat(live_keys, BLK, axis=1), jnp.float32(0.0), jnp.float32(MASKED))
    scores = scores + penalty[:, None, None, :]
    highest = lax.optimization_barrier(jnp.max(scores, axis=-1, keepdims=True))
    raised = jnp.exp(scores - highest)
    weights = (raised / lax.optimization_barrier(jnp.sum(raised, axis=-1, keepdims=True))).astype(jnp.bfloat16)
    output = jnp.einsum('bhqk,bkhd->bqhd', weights.astype(jnp.float32), value_rows.astype(jnp.float32))
    return output.astype(jnp.bfloat16)

def reference(tokens, mod_shift, mod_scale, attn_gate, w_qkv, query_gain, key_gain, w_out, w_dec, conv_weight, block_lists, active_blocks, to_next, to_prev, conv_table):

    def project_group(group_rows):
        return project(group_rows, mod_shift, mod_scale, w_qkv, query_gain, key_gain)
    queries, key_part, values = lax.map(project_group, tokens.reshape(N_SEQ, GB * BLK, D))
    key_blocks = key_part.reshape(NBLOCKS, BLK, HEADS, HD)
    value_blocks = values.reshape(NBLOCKS, BLK, HEADS, HD)
    live_lists = block_flags(block_lists, active_blocks)

    def one_group(inputs):
        query_rows, lists, live_keys = inputs
        picked_keys = key_blocks[lists].reshape(GB, KB * BLK, HEADS, HD)
        picked_values = value_blocks[lists].reshape(GB, KB * BLK, HEADS, HD)
        return attend(query_rows.reshape(GB, BLK, HEADS, HD), picked_keys, picked_values, live_keys)
    attended = lax.map(one_group, (queries, block_lists.reshape(N_SEQ, GB, KB), live_lists.reshape(N_SEQ, GB, KB)))
    attended = attended.reshape(TOKENS, D)
    update = jnp.dot(attended, w_out, preferred_element_type=jnp.float32)
    residual = tokens.astype(jnp.float32) + attn_gate * update
    slot_ids = jnp.arange(TOKENS, dtype=jnp.int32)
    live_rows = slot_ids % TOK_DEV < active_blocks[slot_ids // TOK_DEV] * BLK
    block_out = jnp.where(live_rows[:, None], residual, jnp.float32(0.0)).astype(jnp.bfloat16)
    features = jnp.dot(block_out, w_dec, preferred_element_type=jnp.float32).astype(jnp.bfloat16)
    per_owner = features.reshape(DEVICES, TOK_DEV, C)
    sent_next = jnp.take_along_axis(per_owner, to_next.reshape(DEVICES, FACE)[:, :, None], axis=1)
    sent_prev = jnp.take_along_axis(per_owner, to_prev.reshape(DEVICES, FACE)[:, :, None], axis=1)
    blank_rows = jnp.zeros((1, FACE, C), jnp.bfloat16)
    from_prev = jnp.concatenate([blank_rows, sent_next[:-1]], axis=0)
    from_next = jnp.concatenate([sent_prev[1:], blank_rows], axis=0)
    buffers = jnp.concatenate([per_owner, from_prev, from_next, jnp.zeros((DEVICES, 1, C), jnp.bfloat16)], axis=1)

    def convolve(inputs):
        buffer, offsets = inputs
        tap_rows = buffer[offsets].reshape(TOK_DEV, TAPS * C)
        return jnp.dot(tap_rows, conv_weight, preferred_element_type=jnp.float32)
    conv_out = lax.map(convolve, (buffers, conv_table.reshape(DEVICES, TOK_DEV, TAPS))).reshape(TOKENS, C)
    decoded = jnp.where(live_rows[:, None], features.astype(jnp.float32) + conv_out, jnp.float32(0.0)).astype(jnp.bfloat16)
    return (block_out, decoded)
```

```python
import functools
import math

import jax
import jax.numpy as jnp
from jax import lax
from jax.experimental import pallas as pl
from jax.experimental.pallas import tpu as pltpu
from jax.sharding import PartitionSpec as P

HD = 64
BLK = 64
NB = 8
KB = 8
NC = 4
EPSILON = 1e-06
MASKED = -1000000000.0
MESH = pl.DeviceIdType.MESH
BF16 = jnp.bfloat16
F32 = jnp.float32


def block_kernel(
    S, H,
    tokens, mod_shift, mod_scale, q_gain, k_gain, attn_gate, to_next, to_prev, lists, active,
    w_qkv, w_out, w_dec, conv_w,
    block_out, pieces, conv_wt,
    arr, keys, vals, q, wq, wk, wv, wvt, wo, wd, wdt, wc, own_o, send_o, recv_o, out_rows, chosen, face, face_in,
    w_sem, out_sem, rsem, sx, sy, sf, s1, s2, o_ssem, o_rsem, face_ssem, face_rsem,
):
    T, D = tokens.shape
    W = D // 2
    X = H // 2
    half = H // 2
    CH = T // NC
    CB = CH // BLK
    early = NC // 2
    s = lax.axis_index("seq")
    h = lax.axis_index("head")
    x, c = h // 2, h % 2
    device = s * H + h
    has_next, has_prev = s < S - 1, s > 0
    ahead = 2 * x >= half

    def seq_exists(ahead_of):
        return jnp.logical_or(
            jnp.logical_and(ahead_of, has_next), jnp.logical_and(jnp.logical_not(ahead_of), has_prev)
        )

    def halo_exists(ahead_of):
        return jnp.logical_or(
            jnp.logical_and(ahead_of, has_prev), jnp.logical_and(jnp.logical_not(ahead_of), has_next)
        )

    def seq_target(ahead_of):
        return jnp.where(ahead_of, s + 1, s - 1)

    def own_slot(xx, cc):
        return half + 2 * xx + cc

    def halo_slot(xx, cc):
        return jnp.where(2 * xx >= half, 2 * xx + cc - half, half + H + 2 * xx + cc)

    any_next, any_prev = device < S * H - 1, device > 0
    cross_next = jnp.logical_and(c == 1, any_next)
    cross_prev = jnp.logical_and(c == 0, any_prev)
    next_id = ((device + 1) // H, (device + 1) % H)
    prev_id = ((device + S * H - 1) // H % S, (device + H - 1) % H)

    one, none = jnp.int32(1), jnp.int32(0)
    barrier = pltpu.get_barrier_semaphore()
    for dx in range(1, X):
        pl.semaphore_signal(
            barrier, inc=1, device_id=(s, 2 * ((x + dx) % X) + c), device_id_type=MESH
        )
    pl.semaphore_signal(barrier, inc=1, device_id=(s, 2 * x + 1 - c), device_id_type=MESH)
    for cond, where in (
        (has_next, (s + 1, h)), (has_prev, (s - 1, h)), (cross_next, next_id), (cross_prev, prev_id)
    ):
        @pl.when(cond)
        def _():
            pl.semaphore_signal(barrier, inc=1, device_id=where, device_id_type=MESH)

    mine = pl.multiple_of(c * W, W)
    other = pl.multiple_of((1 - c) * W, W)
    loads = [
        pltpu.make_async_copy(w_qkv.at[:, pl.ds(pl.multiple_of(n * D + c * W, W), W)], ref, w_sem.at[n])
        for n, ref in enumerate((wq, wk, wv))
    ]
    loads.append(pltpu.make_async_copy(w_dec, wd, w_sem.at[3]))
    loads.append(pltpu.make_async_copy(w_out, wo, w_sem.at[4]))
    loads.append(pltpu.make_async_copy(conv_w, wc, w_sem.at[5]))
    for load in loads:
        load.start()

    def chunk(slot, k):
        return arr.at[slot, pl.ds(pl.multiple_of(k * CH, CH), CH), :]

    def remote(src, dst, ssem, recv, target):
        return pltpu.make_async_remote_copy(
            src_ref=src, dst_ref=dst, send_sem=ssem, recv_sem=recv, device_id=target, device_id_type=MESH
        )

    me = own_slot(x, c)

    def send_x(dx, k):
        return remote(chunk(me, k), chunk(me, k), sx.at[dx, k], rsem.at[me, k], (s, 2 * ((x + dx) % X) + c))

    def send_seq(k):
        slot = halo_slot(x, c)
        return remote(chunk(me, k), chunk(slot, k), sy.at[k], rsem.at[slot, k], (seq_target(ahead), h))

    def forward(slot, k):
        return remote(
            chunk(slot, k), chunk(slot, k), sf.at[slot // 2, k], rsem.at[slot, k], (s, 2 * x + 1 - c)
        )

    def relay_seq(dx, k):
        xx = (x + dx) % X
        slot = halo_slot(xx, c)
        return remote(
            chunk(own_slot(xx, c), k), chunk(slot, k), s1.at[dx, k], rsem.at[slot, k],
            (seq_target(2 * xx >= half), h),
        )

    def relay_x(dx, k):
        slot = halo_slot(x, c)
        return remote(
            chunk(slot, k), chunk(slot, k), s2.at[dx, k - early], rsem.at[slot, k],
            (s, 2 * ((x + dx) % X) + c),
        )

    def arrived(slot, k):
        ref = chunk(slot, k)
        pltpu.make_async_copy(ref, ref, rsem.at[slot, k]).wait()

    RT = 64

    def norm_rows(r):
        rows = pl.ds(pl.multiple_of(r * RT, RT), RT)
        v = tokens[rows, :].astype(F32)
        centred = v - jnp.mean(v, axis=-1, keepdims=True)
        spread = jnp.mean(centred * centred, axis=-1, keepdims=True)
        y = centred * lax.rsqrt(spread + EPSILON) * (1.0 + mod_scale[...]) + mod_shift[...]
        arr[me, rows, :] = y.astype(BF16)

    def send_own(k):
        @pl.when(k < early)
        def _():
            for dx in range(1, X):
                send_x(dx, k).start()

        @pl.when(jnp.logical_and(k >= early, seq_exists(ahead)))
        def _():
            send_seq(k).start()

        forward(me, k).start()

    def send_late(k):
        for dx in range(1, X):
            send_x(dx, k).wait_send()
            send_x(dx, k + early).start()

        @pl.when(seq_exists(ahead))
        def _():
            send_seq(k + early).wait_send()
            send_seq(k).start()

    def norm_chunk(k):
        lax.fori_loop(0, CH // RT, lambda r, _: (norm_rows(k * (CH // RT) + r), 0)[1], 0)

    def start_chunk(n, _):
        k = (n % 2) * early + n // 2
        norm_chunk(k)

        @pl.when(n == 0)
        def _():
            peers = X
            for cond in (has_next, has_prev, cross_next, cross_prev):
                peers = peers + jnp.where(cond, one, none)
            pl.semaphore_wait(barrier, peers)

        send_own(k)
        return 0

    lax.fori_loop(0, NC, start_chunk, 0)

    WT = min(256, W)
    same = (
        lax.broadcasted_iota(jnp.int32, (WT, WT), 0) // HD
        == lax.broadcasted_iota(jnp.int32, (WT, WT), 1) // HD
    )
    averaging = jnp.where(same, F32(1.0 / HD), F32(0.0)).astype(BF16)
    averaging = jnp.concatenate([averaging, averaging], axis=0)

    def head_norm(v, gain):
        square = v * v
        high = square.astype(BF16)
        low = (square - high.astype(F32)).astype(BF16)
        parts = []
        for n in range(v.shape[1] // WT):
            cols = slice(n * WT, (n + 1) * WT)
            both = jnp.concatenate([high[:, cols], low[:, cols]], axis=1)
            mean = jnp.dot(both, averaging, preferred_element_type=F32)
            parts.append(v[:, cols] * lax.rsqrt(mean + EPSILON))
        return jnp.concatenate(parts, axis=1) * gain

    def unit_rows(slot0, k):
        rows = pl.ds(pl.multiple_of(k * CH, CH), CH)
        return jnp.concatenate([arr[slot0, rows, :], arr[slot0 + 1, rows, :]], axis=0)

    swap = lax.broadcasted_iota(jnp.int32, (W, 2 * BLK), 1) < BLK

    def make_kv(slot0, k):
        v = unit_rows(slot0, k)
        key = head_norm(
            jnp.dot(v, wk[...], preferred_element_type=F32), k_gain[:, pl.ds(mine, W)]
        ).astype(BF16)
        val = lax.dot_general(wvt[...], v, (((1,), (1,)), ((), ())), preferred_element_type=F32)
        for n in range(2):
            first = (slot0 + n) * NB + k * CB
            keys[pl.ds(first, CB)] = key[n * CH : (n + 1) * CH].reshape(CB, BLK, W)
            for m in range(CB // 2):
                pair = val[:, n * CH + m * 2 * BLK : n * CH + (m + 1) * 2 * BLK]
                turned = pltpu.roll(pair, BLK, 1)
                vals[first + 2 * m] = jnp.where(swap, pair, turned).astype(BF16)
                vals[first + 2 * m + 1] = jnp.where(swap, turned, pair).astype(BF16)

    def make_q(slot0, k):
        v = unit_rows(slot0, k)
        query = head_norm(
            jnp.dot(v, wq[...], preferred_element_type=F32), q_gain[:, pl.ds(mine, W)]
        ).astype(BF16)
        query = query * jnp.asarray(1.0 / math.sqrt(HD), BF16)
        for n in range(2):
            q[pl.ds(n * NB + k * CB, CB)] = query[n * CH : (n + 1) * CH].reshape(CB, BLK, W)

    spots = lax.broadcasted_iota(jnp.int32, (T, to_next.shape[1]), 0)
    for n, ref in enumerate((to_next, to_prev)):
        chosen[n] = jnp.where(spots == ref[...], F32(1.0), F32(0.0)).astype(BF16)
    for load in loads:
        load.wait()
    wdt[...] = wd[...].T

    def turn_values(n, _):
        rows = pl.ds(pl.multiple_of(n * 128, 128), 128)
        wvt[:, rows] = wv[rows, :].T
        return 0

    lax.fori_loop(0, D // 128, turn_values, 0)
    C = w_dec.shape[1]

    def turn_taps(n, _):
        rows = pl.ds(pl.multiple_of(n * C, C), C)
        conv_wt[:, rows] = wc[rows, :].T
        return 0

    lax.fori_loop(0, conv_w.shape[0] // C, turn_taps, 0)

    def relay_step(k):
        def peer(dx, _):
            xx = (x + dx) % X
            slot = own_slot(xx, c)
            arrived(slot, k)

            @pl.when(jnp.logical_and(k < early, seq_exists(2 * xx >= half)))
            def _():
                relay_seq(dx, k).start()

            forward(slot, k).start()
            return 0

        lax.fori_loop(1, X, peer, 0)
        k2 = (k + early) % NC

        @pl.when(halo_exists(ahead))
        def _():
            slot = halo_slot(x, c)
            arrived(slot, k2)

            @pl.when(k2 >= early)
            def _():
                for dx in range(1, X):
                    relay_x(dx, k2).start()

            forward(slot, k2).start()

    def own_step(k, _):
        arrived(own_slot(x, 1 - c), k)
        make_q(own_slot(x, 0), k)
        make_kv(own_slot(x, 0), k)

        @pl.when(k % 2 == 1)
        def _():
            send_late(k // 2)
            relay_step(k // 2)

        return 0

    lax.fori_loop(0, NC, own_step, 0)

    def direct_step(k, _):
        @pl.when(k >= early)
        def _():
            relay_step(k)

        def work(dx, _):
            xx = (x + dx) % X
            arrived(own_slot(xx, 1 - c), k)
            make_kv(own_slot(xx, 0), k)
            return 0

        lax.fori_loop(1, X, work, 0)

        @pl.when(halo_exists(ahead))
        def _():
            k2 = (k + early) % NC
            arrived(halo_slot(x, 1 - c), k2)
            make_kv(halo_slot(x, 0), k2)

        return 0

    lax.fori_loop(0, NC, direct_step, 0)

    def diagonal_step(m, _):
        def pass_on(n, _):
            xx, k = (x + 1 + n // 2) % X, (n % 2) * early + m

            @pl.when(halo_exists(2 * xx >= half))
            def _():
                slot = halo_slot(xx, c)
                arrived(slot, k)
                forward(slot, k).start()

            return 0

        def work(n, _):
            xx, k = (x + 1 + n // 2) % X, (n % 2) * early + m

            @pl.when(halo_exists(2 * xx >= half))
            def _():
                arrived(halo_slot(xx, 1 - c), k)
                make_kv(halo_slot(xx, 0), k)

            return 0

        lax.fori_loop(0, 2 * (X - 1), pass_on, 0)
        lax.fori_loop(0, 2 * (X - 1), work, 0)
        return 0

    lax.fori_loop(0, early, diagonal_step, 0)

    G = WT // HD
    base = (s * H - half) * NB
    diagonal = jnp.where(
        lax.broadcasted_iota(jnp.int32, (G * BLK, WT), 0) // BLK
        == lax.broadcasted_iota(jnp.int32, (G * BLK, WT), 1) // HD,
        F32(1.0), F32(0.0),
    ).astype(BF16)
    low = lax.broadcasted_iota(jnp.int32, (WT, 2 * BLK), 1) < BLK
    head_of = lax.broadcasted_iota(jnp.int32, (HD, G * BLK), 1) // BLK

    def attend(core, b, dst):
        row = (2 * x + core) * NB + b
        local, penalty = [], []
        for n in range(KB):
            block = lists[n, row]
            live = lax.rem(block, NB) < active[block // NB]
            penalty.append(jnp.where(live, F32(0.0), F32(MASKED)))
            local.append(jnp.clip(block - base, 0, 2 * H * NB - 1))
        for g in range(W // WT):
            cols = slice(g * WT, (g + 1) * WT)
            spread = jnp.concatenate([q[core * NB + b, :, cols]] * G, axis=0) * diagonal
            key = jnp.concatenate([keys[l, :, cols] for l in local], axis=0)
            scores = lax.dot_general(key, spread, (((1,), (1,)), ((), ())), preferred_element_type=F32)
            scores = [scores[n * BLK : (n + 1) * BLK] for n in range(KB)]
            highest = functools.reduce(
                jnp.maximum, [jnp.max(v, axis=0, keepdims=True) + p for v, p in zip(scores, penalty)]
            )
            raised = [jnp.exp(v - (highest - p)) for v, p in zip(scores, penalty)]
            total = functools.reduce(jnp.add, [jnp.sum(v, axis=0, keepdims=True) for v in raised])
            scale = 1.0 / total
            weights = jnp.concatenate([(v * scale).astype(BF16) for v in raised], axis=0)
            value = jnp.concatenate(
                [
                    jnp.where(low, vals[local[n], cols, :], vals[local[n + 1], cols, :])
                    for n in range(0, KB, 2)
                ],
                axis=1,
            )
            mixed = jnp.dot(value, weights, preferred_element_type=F32)
            result = mixed[0:HD]
            for n in range(1, G):
                result = jnp.where(head_of == n, mixed[n * HD : (n + 1) * HD], result)
            result = result.T
            dst[pl.ds(pl.multiple_of(b * BLK, BLK), BLK), cols] = jnp.concatenate(
                [result[n * BLK : (n + 1) * BLK] for n in range(G)], axis=1
            ).astype(BF16)

    def attend_all(core, dst):
        def step(n, _):
            for m in range(4):
                attend(core, 4 * n + m, dst)
            return 0

        lax.fori_loop(0, NB // 4, step, 0)

    def o_copy():
        return remote(send_o, recv_o, o_ssem, o_rsem, (s, 2 * x + 1 - c))

    attend_all(1 - c, send_o)
    o_copy().start()
    attend_all(c, own_o)
    o_copy().wait_recv()

    own_live = active[device] * BLK
    OR = min(256, T)
    OC = min(256, D)

    def project_out(n, _):
        r, j = n // (D // OC), n % (D // OC)
        rows = pl.ds(pl.multiple_of(r * OR, OR), OR)
        cols = pl.ds(pl.multiple_of(j * OC, OC), OC)
        update = jnp.dot(own_o[rows, :], wo[pl.ds(mine, W), cols], preferred_element_type=F32) + jnp.dot(
            recv_o[rows, :], wo[pl.ds(other, W), cols], preferred_element_type=F32
        )
        live = lax.broadcasted_iota(jnp.int32, (OR, 1), 0) + r * OR < own_live
        residual = tokens[rows, cols].astype(F32) + attn_gate[:, cols] * update
        out_rows[rows, cols] = jnp.where(live, residual, 0.0).astype(BF16)
        return 0

    lax.fori_loop(0, (T // OR) * (D // OC), project_out, 0)
    out_copy = pltpu.make_async_copy(out_rows, block_out, out_sem)
    out_copy.start()
    features = lax.dot_general(
        wdt[...], out_rows[...], (((1,), (1,)), ((), ())), preferred_element_type=F32
    ).astype(BF16)
    for n in range(2):
        face[n] = jnp.dot(features, chosen[n], preferred_element_type=F32).astype(BF16)

    def face_copy(n, target):
        return remote(face.at[n], face_in.at[n], face_ssem.at[n], face_rsem.at[n], target)

    @pl.when(any_next)
    def _():
        face_copy(0, next_id).start()

    @pl.when(any_prev)
    def _():
        face_copy(1, prev_id).start()

    FACE = to_next.shape[1]
    SEG = pieces.shape[2]
    for n in range(T // SEG):
        pieces[n] = features[:, n * SEG : (n + 1) * SEG]
    for n, cond in ((0, any_prev), (1, any_next)):
        @pl.when(cond)
        def _():
            pltpu.make_async_copy(face_in.at[n], face_in.at[n], face_rsem.at[n]).wait()
            pieces[T // SEG, :, n * FACE : (n + 1) * FACE] = face_in[n]

        @pl.when(jnp.logical_not(cond))
        def _():
            pieces[T // SEG, :, n * FACE : (n + 1) * FACE] = jnp.zeros((pieces.shape[1], FACE), BF16)

    out_copy.wait()
    o_copy().wait_send()

    @pl.when(any_next)
    def _():
        face_copy(0, next_id).wait_send()

    @pl.when(any_prev)
    def _():
        face_copy(1, prev_id).wait_send()

    def drain(k, _):
        forward(me, k).wait_send()

        @pl.when(jnp.logical_and(k < early, seq_exists(ahead)))
        def _():
            send_seq(k).wait_send()

        @pl.when(halo_exists(ahead))
        def _():
            forward(halo_slot(x, c), k).wait_send()

            @pl.when(k >= early)
            def _():
                for dx in range(1, X):
                    relay_x(dx, k).wait_send()

        def peer(dx, _):
            xx = (x + dx) % X
            forward(own_slot(xx, c), k).wait_send()

            @pl.when(k >= early)
            def _():
                send_x(dx, k).wait_send()

            @pl.when(jnp.logical_and(k < early, seq_exists(2 * xx >= half)))
            def _():
                relay_seq(dx, k).wait_send()

            @pl.when(halo_exists(2 * xx >= half))
            def _():
                forward(halo_slot(xx, c), k).wait_send()

            return 0

        lax.fori_loop(1, X, peer, 0)
        return 0

    lax.fori_loop(0, NC, drain, 0)


def conv_kernel(block_in, pieces, table, conv_wt, active, block_out, decoded, held, gathered, sem):
    fetch = pltpu.make_async_copy(block_in, held, sem.at[0])
    store = pltpu.make_async_copy(held, block_out, sem.at[1])
    fetch.start()
    N, C, SEG = pieces.shape
    TAPS, T = table.shape
    device = lax.axis_index("seq") * lax.axis_size("head") + lax.axis_index("head")
    spots = lax.broadcasted_iota(jnp.int32, (SEG, T), 0).astype(F32).astype(BF16)
    stacked = pieces[...].reshape(N * C, SEG)

    def gather(t):
        index = table[pl.ds(t, 1), :]
        segment = index // SEG
        offset = (index - segment * SEG).astype(F32).astype(BF16)
        onehot = jnp.where(spots == offset, BF16(1.0), BF16(0.0))
        found = jnp.dot(stacked, onehot, preferred_element_type=F32).astype(BF16)
        rows = jnp.zeros((C, T), BF16)
        for n in range(N):
            rows = jnp.where(segment == n, found[n * C : (n + 1) * C], rows)
        gathered[pl.ds(pl.multiple_of(t * C, C), C), :] = rows

    U = 9 if TAPS % 9 == 0 else 1

    def step(n, _):
        for m in range(U):
            gather(U * n + m)
        return 0

    lax.fori_loop(0, TAPS // U, step, 0)
    fetch.wait()
    store.start()
    own = jnp.concatenate([pieces[n] for n in range(T // SEG)], axis=1).astype(F32)
    total = own + jnp.dot(conv_wt[...], gathered[...], preferred_element_type=F32)
    live = lax.broadcasted_iota(jnp.int32, (1, T), 1) < active[device] * BLK
    decoded[...] = jnp.where(live, total, 0.0).T.astype(BF16)
    store.wait()


def body(
    tokens, mod_shift, mod_scale, attn_gate, w_qkv, query_gain, key_gain, w_out, w_dec,
    conv_weight, block_lists, active_blocks, to_next, to_prev, conv_table,
):
    S, H = lax.axis_size("seq"), lax.axis_size("head")
    T, D = tokens.shape
    W = D // 2
    X = H // 2
    C = w_dec.shape[1]
    taps = conv_table.shape[1]
    face = to_next.shape[0]
    seg = 2 * face
    vmem = pl.BlockSpec(memory_space=pltpu.VMEM)
    smem = pl.BlockSpec(memory_space=pltpu.SMEM)
    hbm = pl.BlockSpec(memory_space=pl.ANY)
    dma = pltpu.SemaphoreType.DMA
    grant = 60 * 1024 * 1024
    rows, pieces, conv_wt = pl.pallas_call(
        functools.partial(block_kernel, S, H),
        out_shape=(
            jax.ShapeDtypeStruct((T, D), BF16),
            jax.ShapeDtypeStruct((T // seg + 1, C, seg), BF16),
            jax.ShapeDtypeStruct((C, taps * C), BF16),
        ),
        in_specs=[vmem] * 8 + [smem] * 2 + [hbm] * 4,
        out_specs=(hbm, vmem, vmem),
        scratch_shapes=[
            pltpu.VMEM((2 * H, T, D), BF16),
            pltpu.VMEM((2 * H * NB, BLK, W), BF16),
            pltpu.VMEM((2 * H * NB, W, 2 * BLK), BF16),
            pltpu.VMEM((2 * NB, BLK, W), BF16),
            pltpu.VMEM((D, W), BF16),
            pltpu.VMEM((D, W), BF16),
            pltpu.VMEM((D, W), BF16),
            pltpu.VMEM((W, D), BF16),
            pltpu.VMEM((D, D), BF16),
            pltpu.VMEM((D, C), BF16),
            pltpu.VMEM((C, D), BF16),
            pltpu.VMEM((taps * C, C), BF16),
            pltpu.VMEM((T, W), BF16),
            pltpu.VMEM((T, W), BF16),
            pltpu.VMEM((T, W), BF16),
            pltpu.VMEM((T, D), BF16),
            pltpu.VMEM((2, T, face), BF16),
            pltpu.VMEM((2, C, face), BF16),
            pltpu.VMEM((2, C, face), BF16),
            dma((6,)), dma, dma((2 * H, NC)), dma((X, NC)), dma((NC,)), dma((H, NC)),
            dma((X, NC // 2)), dma((X, NC // 2)), dma, dma, dma((2,)), dma((2,)),
        ],
        compiler_params=pltpu.CompilerParams(
            collective_id=0, has_side_effects=True, vmem_limit_bytes=grant
        ),
    )(
        tokens, mod_shift.reshape(1, D), mod_scale.reshape(1, D), query_gain.reshape(1, D),
        key_gain.reshape(1, D), attn_gate.reshape(1, D), to_next.reshape(1, face),
        to_prev.reshape(1, face), block_lists.T, active_blocks, w_qkv, w_out, w_dec,
        conv_weight,
    )
    return pl.pallas_call(
        conv_kernel,
        out_shape=(
            jax.ShapeDtypeStruct((T, D), BF16),
            jax.ShapeDtypeStruct((T, C), BF16),
        ),
        in_specs=[hbm, vmem, vmem, vmem, smem],
        out_specs=(hbm, vmem),
        scratch_shapes=[
            pltpu.VMEM((T, D), BF16), pltpu.VMEM((taps * C, T), BF16), dma((2,)),
        ],
        compiler_params=pltpu.CompilerParams(vmem_limit_bytes=grant),
    )(rows, pieces, conv_table.T, conv_wt, active_blocks)


def solution(mesh):
    rows = P(("seq", "head"), None)
    return jax.shard_map(
        body,
        mesh=mesh,
        in_specs=(
            rows, P(), P(), P(), P(), P(), P(), P(), P(), P(),
            P("seq", None), P(), P(("seq", "head")), P(("seq", "head")), rows,
        ),
        out_specs=(rows, rows),
        check_vma=False,
    )
```

```python
import functools
import math

import jax
import jax.numpy as jnp
from jax import lax
from jax.experimental import pallas as pl
from jax.experimental.pallas import tpu as pltpu
from jax.sharding import PartitionSpec as P

HD = 64
BLK = 64
NB = 8
KB = 8
NC = 4
EPSILON = 1e-06
MASKED = -1000000000.0
MESH = pl.DeviceIdType.MESH
BF16 = jnp.bfloat16
F32 = jnp.float32


def block_kernel(
    S, H,
    tokens, mod_shift, mod_scale, q_gain, k_gain, attn_gate, to_next, to_prev, lists, active,
    w_qkv, w_out, w_dec, conv_w,
    block_out, pieces, conv_wt,
    arr, keys, vals, q, wq, wk, wv, wvt, wo, wd, wdt, wc, own_o, send_o, recv_o, out_rows, chosen, face, face_in,
    w_sem, out_sem, rsem, sx, sy, sf, s1, s2, o_ssem, o_rsem, face_ssem, face_rsem,
):
    T, D = tokens.shape
    W = D // 2
    X = H // 2
    half = H // 2
    CH = T // NC
    CB = CH // BLK
    early = NC // 2
    s = lax.axis_index("seq")
    h = lax.axis_index("head")
    x, c = h // 2, h % 2
    device = s * H + h
    has_next, has_prev = s < S - 1, s > 0
    ahead = 2 * x >= half

    def seq_exists(ahead_of):
        return jnp.logical_or(
            jnp.logical_and(ahead_of, has_next), jnp.logical_and(jnp.logical_not(ahead_of), has_prev)
        )

    def halo_exists(ahead_of):
        return jnp.logical_or(
            jnp.logical_and(ahead_of, has_prev), jnp.logical_and(jnp.logical_not(ahead_of), has_next)
        )

    def seq_target(ahead_of):
        return jnp.where(ahead_of, s + 1, s - 1)

    def own_slot(xx, cc):
        return half + 2 * xx + cc

    def halo_slot(xx, cc):
        return jnp.where(2 * xx >= half, 2 * xx + cc - half, half + H + 2 * xx + cc)

    any_next, any_prev = device < S * H - 1, device > 0
    cross_next = jnp.logical_and(c == 1, any_next)
    cross_prev = jnp.logical_and(c == 0, any_prev)
    next_id = ((device + 1) // H, (device + 1) % H)
    prev_id = ((device + S * H - 1) // H % S, (device + H - 1) % H)

    one, none = jnp.int32(1), jnp.int32(0)
    barrier = pltpu.get_barrier_semaphore()
    for dx in range(1, X):
        pl.semaphore_signal(
            barrier, inc=1, device_id=(s, 2 * ((x + dx) % X) + c), device_id_type=MESH
        )
    pl.semaphore_signal(barrier, inc=1, device_id=(s, 2 * x + 1 - c), device_id_type=MESH)
    for cond, where in (
        (has_next, (s + 1, h)), (has_prev, (s - 1, h)), (cross_next, next_id), (cross_prev, prev_id)
    ):
        @pl.when(cond)
        def _():
            pl.semaphore_signal(barrier, inc=1, device_id=where, device_id_type=MESH)

    mine = pl.multiple_of(c * W, W)
    other = pl.multiple_of((1 - c) * W, W)
    loads = [
        pltpu.make_async_copy(w_qkv.at[:, pl.ds(pl.multiple_of(n * D + c * W, W), W)], ref, w_sem.at[n])
        for n, ref in enumerate((wq, wk, wv))
    ]
    loads.append(pltpu.make_async_copy(w_dec, wd, w_sem.at[3]))
    loads.append(pltpu.make_async_copy(w_out, wo, w_sem.at[4]))
    loads.append(pltpu.make_async_copy(conv_w, wc, w_sem.at[5]))
    for load in loads:
        load.start()

    def chunk(slot, k):
        return arr.at[slot, pl.ds(pl.multiple_of(k * CH, CH), CH), :]

    def remote(src, dst, ssem, recv, target):
        return pltpu.make_async_remote_copy(
            src_ref=src, dst_ref=dst, send_sem=ssem, recv_sem=recv, device_id=target, device_id_type=MESH
        )

    me = own_slot(x, c)

    def send_x(dx, k):
        return remote(chunk(me, k), chunk(me, k), sx.at[dx, k], rsem.at[me, k], (s, 2 * ((x + dx) % X) + c))

    def send_seq(k):
        slot = halo_slot(x, c)
        return remote(chunk(me, k), chunk(slot, k), sy.at[k], rsem.at[slot, k], (seq_target(ahead), h))

    def forward(slot, k):
        return remote(
            chunk(slot, k), chunk(slot, k), sf.at[slot // 2, k], rsem.at[slot, k], (s, 2 * x + 1 - c)
        )

    def relay_seq(dx, k):
        xx = (x + dx) % X
        slot = halo_slot(xx, c)
        return remote(
            chunk(own_slot(xx, c), k), chunk(slot, k), s1.at[dx, k], rsem.at[slot, k],
            (seq_target(2 * xx >= half), h),
        )

    def relay_x(dx, k):
        slot = halo_slot(x, c)
        return remote(
            chunk(slot, k), chunk(slot, k), s2.at[dx, k - early], rsem.at[slot, k],
            (s, 2 * ((x + dx) % X) + c),
        )

    def arrived(slot, k):
        ref = chunk(slot, k)
        pltpu.make_async_copy(ref, ref, rsem.at[slot, k]).wait()

    RT = min(128, CH)

    def norm_rows(r):
        rows = pl.ds(pl.multiple_of(r * RT, RT), RT)
        v = tokens[rows, :].astype(F32)
        centred = v - jnp.mean(v, axis=-1, keepdims=True)
        spread = jnp.mean(centred * centred, axis=-1, keepdims=True)
        y = centred * lax.rsqrt(spread + EPSILON) * (1.0 + mod_scale[...]) + mod_shift[...]
        arr[me, rows, :] = y.astype(BF16)

    def send_first(k):
        for dx in range(1, X):
            send_x(dx, k).start()

    def send_halo(k):
        @pl.when(seq_exists(ahead))
        def _():
            send_seq(k).start()

    def norm_chunk(k):
        lax.fori_loop(0, CH // RT, lambda r, _: (norm_rows(k * (CH // RT) + r), 0)[1], 0)

    def start_chunk(n, _):
        k = (n % 2) * early + n // 2
        norm_chunk(k)

        @pl.when(n == 0)
        def _():
            peers = X
            for cond in (has_next, has_prev, cross_next, cross_prev):
                peers = peers + jnp.where(cond, one, none)
            pl.semaphore_wait(barrier, peers)

        @pl.when(n == 0)
        def _():
            send_first(0)

        @pl.when(n == 1)
        def _():
            send_halo(early)

        forward(me, k).start()
        return 0

    lax.fori_loop(0, NC, start_chunk, 0)

    WT = min(256, W)
    same = (
        lax.broadcasted_iota(jnp.int32, (WT, WT), 0) // HD
        == lax.broadcasted_iota(jnp.int32, (WT, WT), 1) // HD
    )
    averaging = jnp.where(same, F32(1.0 / HD), F32(0.0)).astype(BF16)
    averaging = jnp.concatenate([averaging, averaging], axis=0)

    def head_norm(v, gain):
        square = v * v
        high = square.astype(BF16)
        low = (square - high.astype(F32)).astype(BF16)
        parts = []
        for n in range(v.shape[1] // WT):
            cols = slice(n * WT, (n + 1) * WT)
            both = jnp.concatenate([high[:, cols], low[:, cols]], axis=1)
            mean = jnp.dot(both, averaging, preferred_element_type=F32)
            parts.append(v[:, cols] * lax.rsqrt(mean + EPSILON))
        return jnp.concatenate(parts, axis=1) * gain

    def unit_rows(slot0, k):
        rows = pl.ds(pl.multiple_of(k * CH, CH), CH)
        return jnp.concatenate([arr[slot0, rows, :], arr[slot0 + 1, rows, :]], axis=0)

    swap = lax.broadcasted_iota(jnp.int32, (W, 2 * BLK), 1) < BLK

    def make_kv(slot0, k):
        v = unit_rows(slot0, k)
        key = head_norm(
            jnp.dot(v, wk[...], preferred_element_type=F32), k_gain[:, pl.ds(mine, W)]
        ).astype(BF16)
        val = lax.dot_general(wvt[...], v, (((1,), (1,)), ((), ())), preferred_element_type=F32)
        for n in range(2):
            first = (slot0 + n) * NB + k * CB
            keys[pl.ds(first, CB)] = key[n * CH : (n + 1) * CH].reshape(CB, BLK, W)
            for m in range(CB // 2):
                pair = val[:, n * CH + m * 2 * BLK : n * CH + (m + 1) * 2 * BLK]
                turned = pltpu.roll(pair, BLK, 1)
                vals[first + 2 * m] = jnp.where(swap, pair, turned).astype(BF16)
                vals[first + 2 * m + 1] = jnp.where(swap, turned, pair).astype(BF16)

    def make_q(slot0, k):
        v = unit_rows(slot0, k)
        query = head_norm(
            jnp.dot(v, wq[...], preferred_element_type=F32), q_gain[:, pl.ds(mine, W)]
        ).astype(BF16)
        query = query * jnp.asarray(1.0 / math.sqrt(HD), BF16)
        for n in range(2):
            q[pl.ds(n * NB + k * CB, CB)] = query[n * CH : (n + 1) * CH].reshape(CB, BLK, W)

    spots = lax.broadcasted_iota(jnp.int32, (T, to_next.shape[1]), 0)
    for n, ref in enumerate((to_next, to_prev)):
        chosen[n] = jnp.where(spots == ref[...], F32(1.0), F32(0.0)).astype(BF16)
    for load in loads:
        load.wait()
    wdt[...] = wd[...].T

    def turn_values(n, _):
        rows = pl.ds(pl.multiple_of(n * 128, 128), 128)
        wvt[:, rows] = wv[rows, :].T
        return 0

    lax.fori_loop(0, D // 128, turn_values, 0)
    C = w_dec.shape[1]

    def turn_taps(n, _):
        rows = pl.ds(pl.multiple_of(n * C, C), C)
        conv_wt[:, rows] = wc[rows, :].T
        return 0

    lax.fori_loop(0, conv_w.shape[0] // C, turn_taps, 0)

    for k in range(1, early):
        send_first(k)
        send_halo(k + early)

    def own_step(k, _):
        arrived(own_slot(x, 1 - c), k)
        make_q(own_slot(x, 0), k)
        make_kv(own_slot(x, 0), k)
        return 0

    lax.fori_loop(0, NC, own_step, 0)

    def send_next(i):
        def peer(dx, _):
            @pl.when(i < NC)
            def _():
                send_x(dx, i).wait_send()

            @pl.when(i < early)
            def _():
                send_x(dx, i + early).start()

            return 0

        lax.fori_loop(1, X, peer, 0)

        @pl.when(jnp.logical_and(i < NC, seq_exists(ahead)))
        def _():
            send_seq((i + early) % NC).wait_send()

        @pl.when(jnp.logical_and(i < early, seq_exists(ahead)))
        def _():
            send_seq(i).start()

    def receive_step(i, _):
        send_next(i)
        late = i >= NC

        def lane(n, act):
            dx, over_seq = 1 + n // 2, n % 2 == 1
            xx = (x + dx) % X
            far = halo_exists(2 * xx >= half)
            near = jnp.where(over_seq, jnp.logical_and(dx == 1, halo_exists(ahead)), True)
            k = jnp.where(
                late,
                jnp.where(over_seq, i - NC, i - NC + early),
                jnp.where(over_seq, (i + early) % NC, i),
            )
            slot = jnp.where(
                late, halo_slot(xx, 0), jnp.where(over_seq, halo_slot(x, 0), own_slot(xx, 0))
            )

            @pl.when(jnp.logical_or(jnp.logical_and(late, far), jnp.logical_and(jnp.logical_not(late), near)))
            def _():
                act(slot, k)

        def pass_on(slot, k):
            arrived(slot + c, k)
            forward(slot + c, k).start()

        def relay(dx, _):
            @pl.when(seq_exists(2 * ((x + dx) % X) >= half))
            def _():
                relay_seq(dx, i).start()

            @pl.when(halo_exists(ahead))
            def _():
                relay_x(dx, i + early).start()

            return 0

        def work(slot, k):
            arrived(slot + 1 - c, k)
            make_kv(slot, k)

        lax.fori_loop(0, 2 * (X - 1), lambda n, _: (lane(n, pass_on), 0)[1], 0)

        @pl.when(i < early)
        def _():
            lax.fori_loop(1, X, relay, 0)

        lax.fori_loop(0, 2 * (X - 1), lambda n, _: (lane(n, work), 0)[1], 0)
        return 0

    lax.fori_loop(0, NC + early, receive_step, 0)

    G = WT // HD
    base = (s * H - half) * NB
    diagonal = jnp.where(
        lax.broadcasted_iota(jnp.int32, (G * BLK, WT), 0) // BLK
        == lax.broadcasted_iota(jnp.int32, (G * BLK, WT), 1) // HD,
        F32(1.0), F32(0.0),
    ).astype(BF16)
    low = lax.broadcasted_iota(jnp.int32, (WT, 2 * BLK), 1) < BLK
    head_of = lax.broadcasted_iota(jnp.int32, (HD, G * BLK), 1) // BLK

    def attend(core, b, dst):
        row = (2 * x + core) * NB + b
        local, penalty = [], []
        for n in range(KB):
            block = lists[n, row]
            live = lax.rem(block, NB) < active[block // NB]
            penalty.append(jnp.where(live, F32(0.0), F32(MASKED)))
            local.append(jnp.clip(block - base, 0, 2 * H * NB - 1))
        for g in range(W // WT):
            cols = slice(g * WT, (g + 1) * WT)
            spread = jnp.concatenate([q[core * NB + b, :, cols]] * G, axis=0) * diagonal
            key = jnp.concatenate([keys[l, :, cols] for l in local], axis=0)
            scores = lax.dot_general(key, spread, (((1,), (1,)), ((), ())), preferred_element_type=F32)
            scores = [scores[n * BLK : (n + 1) * BLK] for n in range(KB)]
            highest = functools.reduce(
                jnp.maximum, [jnp.max(v, axis=0, keepdims=True) + p for v, p in zip(scores, penalty)]
            )
            raised = [jnp.exp(v - (highest - p)) for v, p in zip(scores, penalty)]
            total = functools.reduce(jnp.add, [jnp.sum(v, axis=0, keepdims=True) for v in raised])
            scale = 1.0 / total
            weights = jnp.concatenate([(v * scale).astype(BF16) for v in raised], axis=0)
            value = jnp.concatenate(
                [
                    jnp.where(low, vals[local[n], cols, :], vals[local[n + 1], cols, :])
                    for n in range(0, KB, 2)
                ],
                axis=1,
            )
            mixed = jnp.dot(value, weights, preferred_element_type=F32)
            result = mixed[0:HD]
            for n in range(1, G):
                result = jnp.where(head_of == n, mixed[n * HD : (n + 1) * HD], result)
            result = result.T
            dst[pl.ds(pl.multiple_of(b * BLK, BLK), BLK), cols] = jnp.concatenate(
                [result[n * BLK : (n + 1) * BLK] for n in range(G)], axis=1
            ).astype(BF16)

    def attend_all(core, dst):
        def step(n, _):
            for m in range(8):
                attend(core, 8 * n + m, dst)
            return 0

        lax.fori_loop(0, NB // 8, step, 0)

    def o_copy():
        return remote(send_o, recv_o, o_ssem, o_rsem, (s, 2 * x + 1 - c))

    attend_all(1 - c, send_o)
    o_copy().start()
    attend_all(c, own_o)
    o_copy().wait_recv()

    own_live = active[device] * BLK
    OR = min(512, T)
    OC = min(512, D)

    def project_out(n, _):
        r, j = n // (D // OC), n % (D // OC)
        rows = pl.ds(pl.multiple_of(r * OR, OR), OR)
        cols = pl.ds(pl.multiple_of(j * OC, OC), OC)
        update = jnp.dot(own_o[rows, :], wo[pl.ds(mine, W), cols], preferred_element_type=F32) + jnp.dot(
            recv_o[rows, :], wo[pl.ds(other, W), cols], preferred_element_type=F32
        )
        live = lax.broadcasted_iota(jnp.int32, (OR, 1), 0) + r * OR < own_live
        residual = tokens[rows, cols].astype(F32) + attn_gate[:, cols] * update
        out_rows[rows, cols] = jnp.where(live, residual, 0.0).astype(BF16)
        return 0

    lax.fori_loop(0, (T // OR) * (D // OC), project_out, 0)
    out_copy = pltpu.make_async_copy(out_rows, block_out, out_sem)
    out_copy.start()
    features = lax.dot_general(
        wdt[...], out_rows[...], (((1,), (1,)), ((), ())), preferred_element_type=F32
    ).astype(BF16)
    for n in range(2):
        face[n] = jnp.dot(features, chosen[n], preferred_element_type=F32).astype(BF16)

    def face_copy(n, target):
        return remote(face.at[n], face_in.at[n], face_ssem.at[n], face_rsem.at[n], target)

    @pl.when(any_next)
    def _():
        face_copy(0, next_id).start()

    @pl.when(any_prev)
    def _():
        face_copy(1, prev_id).start()

    FACE = to_next.shape[1]
    SEG = pieces.shape[2]
    for n in range(T // SEG):
        pieces[n] = features[:, n * SEG : (n + 1) * SEG]
    for n, cond in ((0, any_prev), (1, any_next)):
        @pl.when(cond)
        def _():
            pltpu.make_async_copy(face_in.at[n], face_in.at[n], face_rsem.at[n]).wait()
            pieces[T // SEG, :, n * FACE : (n + 1) * FACE] = face_in[n]

        @pl.when(jnp.logical_not(cond))
        def _():
            pieces[T // SEG, :, n * FACE : (n + 1) * FACE] = jnp.zeros((pieces.shape[1], FACE), BF16)

    out_copy.wait()
    o_copy().wait_send()

    @pl.when(any_next)
    def _():
        face_copy(0, next_id).wait_send()

    @pl.when(any_prev)
    def _():
        face_copy(1, prev_id).wait_send()

    def drain(k, _):
        forward(me, k).wait_send()

        @pl.when(halo_exists(ahead))
        def _():
            forward(halo_slot(x, c), k).wait_send()

            @pl.when(k >= early)
            def _():
                for dx in range(1, X):
                    relay_x(dx, k).wait_send()

        def peer(dx, _):
            xx = (x + dx) % X
            forward(own_slot(xx, c), k).wait_send()

            @pl.when(jnp.logical_and(k < early, seq_exists(2 * xx >= half)))
            def _():
                relay_seq(dx, k).wait_send()

            @pl.when(halo_exists(2 * xx >= half))
            def _():
                forward(halo_slot(xx, c), k).wait_send()

            return 0

        lax.fori_loop(1, X, peer, 0)
        return 0

    lax.fori_loop(0, NC, drain, 0)


def conv_kernel(block_in, pieces, table, conv_wt, active, block_out, decoded, held, gathered, sem):
    fetch = pltpu.make_async_copy(block_in, held, sem.at[0])
    store = pltpu.make_async_copy(held, block_out, sem.at[1])
    fetch.start()
    N, C, SEG = pieces.shape
    TAPS, T = table.shape
    device = lax.axis_index("seq") * lax.axis_size("head") + lax.axis_index("head")
    spots = lax.broadcasted_iota(jnp.int32, (SEG, T), 0).astype(F32).astype(BF16)
    stacked = pieces[...].reshape(N * C, SEG)

    def gather(t):
        index = table[pl.ds(t, 1), :]
        segment = index // SEG
        offset = (index - segment * SEG).astype(F32).astype(BF16)
        onehot = jnp.where(spots == offset, BF16(1.0), BF16(0.0))
        found = jnp.dot(stacked, onehot, preferred_element_type=F32).astype(BF16)
        rows = jnp.zeros((C, T), BF16)
        for n in range(N):
            rows = jnp.where(segment == n, found[n * C : (n + 1) * C], rows)
        gathered[pl.ds(pl.multiple_of(t * C, C), C), :] = rows

    U = 9 if TAPS % 9 == 0 else 1

    def step(n, _):
        for m in range(U):
            gather(U * n + m)
        return 0

    lax.fori_loop(0, TAPS // U, step, 0)
    fetch.wait()
    store.start()
    own = jnp.concatenate([pieces[n] for n in range(T // SEG)], axis=1).astype(F32)
    total = own + jnp.dot(conv_wt[...], gathered[...], preferred_element_type=F32)
    live = lax.broadcasted_iota(jnp.int32, (1, T), 1) < active[device] * BLK
    decoded[...] = jnp.where(live, total, 0.0).T.astype(BF16)
    store.wait()


def body(
    tokens, mod_shift, mod_scale, attn_gate, w_qkv, query_gain, key_gain, w_out, w_dec,
    conv_weight, block_lists, active_blocks, to_next, to_prev, conv_table,
):
    S, H = lax.axis_size("seq"), lax.axis_size("head")
    T, D = tokens.shape
    W = D // 2
    X = H // 2
    C = w_dec.shape[1]
    taps = conv_table.shape[1]
    face = to_next.shape[0]
    seg = 2 * face
    vmem = pl.BlockSpec(memory_space=pltpu.VMEM)
    smem = pl.BlockSpec(memory_space=pltpu.SMEM)
    hbm = pl.BlockSpec(memory_space=pl.ANY)
    dma = pltpu.SemaphoreType.DMA
    grant = 60 * 1024 * 1024
    rows, pieces, conv_wt = pl.pallas_call(
        functools.partial(block_kernel, S, H),
        out_shape=(
            jax.ShapeDtypeStruct((T, D), BF16),
            jax.ShapeDtypeStruct((T // seg + 1, C, seg), BF16),
            jax.ShapeDtypeStruct((C, taps * C), BF16),
        ),
        in_specs=[vmem] * 8 + [smem] * 2 + [hbm] * 4,
        out_specs=(hbm, vmem, vmem),
        scratch_shapes=[
            pltpu.VMEM((2 * H, T, D), BF16),
            pltpu.VMEM((2 * H * NB, BLK, W), BF16),
            pltpu.VMEM((2 * H * NB, W, 2 * BLK), BF16),
            pltpu.VMEM((2 * NB, BLK, W), BF16),
            pltpu.VMEM((D, W), BF16),
            pltpu.VMEM((D, W), BF16),
            pltpu.VMEM((D, W), BF16),
            pltpu.VMEM((W, D), BF16),
            pltpu.VMEM((D, D), BF16),
            pltpu.VMEM((D, C), BF16),
            pltpu.VMEM((C, D), BF16),
            pltpu.VMEM((taps * C, C), BF16),
            pltpu.VMEM((T, W), BF16),
            pltpu.VMEM((T, W), BF16),
            pltpu.VMEM((T, W), BF16),
            pltpu.VMEM((T, D), BF16),
            pltpu.VMEM((2, T, face), BF16),
            pltpu.VMEM((2, C, face), BF16),
            pltpu.VMEM((2, C, face), BF16),
            dma((6,)), dma, dma((2 * H, NC)), dma((X, NC)), dma((NC,)), dma((H, NC)),
            dma((X, NC // 2)), dma((X, NC // 2)), dma, dma, dma((2,)), dma((2,)),
        ],
        compiler_params=pltpu.CompilerParams(
            collective_id=0, has_side_effects=True, vmem_limit_bytes=grant
        ),
    )(
        tokens, mod_shift.reshape(1, D), mod_scale.reshape(1, D), query_gain.reshape(1, D),
        key_gain.reshape(1, D), attn_gate.reshape(1, D), to_next.reshape(1, face),
        to_prev.reshape(1, face), block_lists.T, active_blocks, w_qkv, w_out, w_dec,
        conv_weight,
    )
    return pl.pallas_call(
        conv_kernel,
        out_shape=(
            jax.ShapeDtypeStruct((T, D), BF16),
            jax.ShapeDtypeStruct((T, C), BF16),
        ),
        in_specs=[hbm, vmem, vmem, vmem, smem],
        out_specs=(hbm, vmem),
        scratch_shapes=[
            pltpu.VMEM((T, D), BF16), pltpu.VMEM((taps * C, T), BF16), dma((2,)),
        ],
        compiler_params=pltpu.CompilerParams(vmem_limit_bytes=grant),
    )(rows, pieces, conv_table.T, conv_wt, active_blocks)


def solution(mesh):
    rows = P(("seq", "head"), None)
    return jax.shard_map(
        body,
        mesh=mesh,
        in_specs=(
            rows, P(), P(), P(), P(), P(), P(), P(), P(), P(),
            P("seq", None), P(), P(("seq", "head")), P(("seq", "head")), rows,
        ),
        out_specs=(rows, rows),
        check_vma=False,
    )
```

```python
import functools
import math

import jax
import jax.numpy as jnp
from jax import lax
from jax.experimental import pallas as pl
from jax.experimental.pallas import tpu as pltpu
from jax.sharding import PartitionSpec as P

HD = 64
BLK = 64
NB = 8
KB = 8
NC = 4
EPSILON = 1e-06
MASKED = -1000000000.0
MESH = pl.DeviceIdType.MESH
BF16 = jnp.bfloat16
F32 = jnp.float32


def block_kernel(
    S, H,
    tokens, mod_shift, mod_scale, q_gain, k_gain, attn_gate, to_next, to_prev, lists, active,
    w_qkv, w_out, w_dec, conv_w,
    block_out, pieces, conv_wt,
    arr, keys, vals, q, wq, wk, wv, wvt, wo, wd, wdt, wc, own_o, send_o, recv_o, out_rows, chosen, face, face_in,
    w_sem, out_sem, rsem, sx, sy, sf, s1, s2, o_ssem, o_rsem, face_ssem, face_rsem,
):
    T, D = tokens.shape
    W = D // 2
    X = H // 2
    half = H // 2
    CH = T // NC
    CB = CH // BLK
    early = NC // 2
    s = lax.axis_index("seq")
    h = lax.axis_index("head")
    x, c = h // 2, h % 2
    device = s * H + h
    has_next, has_prev = s < S - 1, s > 0
    ahead = 2 * x >= half

    def seq_exists(ahead_of):
        return jnp.logical_or(
            jnp.logical_and(ahead_of, has_next), jnp.logical_and(jnp.logical_not(ahead_of), has_prev)
        )

    def halo_exists(ahead_of):
        return jnp.logical_or(
            jnp.logical_and(ahead_of, has_prev), jnp.logical_and(jnp.logical_not(ahead_of), has_next)
        )

    def seq_target(ahead_of):
        return jnp.where(ahead_of, s + 1, s - 1)

    def own_slot(xx, cc):
        return half + 2 * xx + cc

    def halo_slot(xx, cc):
        return jnp.where(2 * xx >= half, 2 * xx + cc - half, half + H + 2 * xx + cc)

    any_next, any_prev = device < S * H - 1, device > 0
    cross_next = jnp.logical_and(c == 1, any_next)
    cross_prev = jnp.logical_and(c == 0, any_prev)
    next_id = ((device + 1) // H, (device + 1) % H)
    prev_id = ((device + S * H - 1) // H % S, (device + H - 1) % H)

    one, none = jnp.int32(1), jnp.int32(0)
    barrier = pltpu.get_barrier_semaphore()
    for dx in range(1, X):
        pl.semaphore_signal(
            barrier, inc=1, device_id=(s, 2 * ((x + dx) % X) + c), device_id_type=MESH
        )
    pl.semaphore_signal(barrier, inc=1, device_id=(s, 2 * x + 1 - c), device_id_type=MESH)
    for cond, where in (
        (has_next, (s + 1, h)), (has_prev, (s - 1, h)), (cross_next, next_id), (cross_prev, prev_id)
    ):
        @pl.when(cond)
        def _():
            pl.semaphore_signal(barrier, inc=1, device_id=where, device_id_type=MESH)

    mine = pl.multiple_of(c * W, W)
    other = pl.multiple_of((1 - c) * W, W)
    loads = [
        pltpu.make_async_copy(w_qkv.at[:, pl.ds(pl.multiple_of(n * D + c * W, W), W)], ref, w_sem.at[n])
        for n, ref in enumerate((wq, wk, wv))
    ]
    loads.append(pltpu.make_async_copy(w_dec, wd, w_sem.at[3]))
    loads.append(pltpu.make_async_copy(w_out, wo, w_sem.at[4]))
    loads.append(pltpu.make_async_copy(conv_w, wc, w_sem.at[5]))
    for load in loads:
        load.start()

    def chunk(slot, k):
        return arr.at[slot, pl.ds(pl.multiple_of(k * CH, CH), CH), :]

    def remote(src, dst, ssem, recv, target):
        return pltpu.make_async_remote_copy(
            src_ref=src, dst_ref=dst, send_sem=ssem, recv_sem=recv, device_id=target, device_id_type=MESH
        )

    me = own_slot(x, c)

    def send_x(dx, k):
        return remote(chunk(me, k), chunk(me, k), sx.at[dx, k], rsem.at[me, k], (s, 2 * ((x + dx) % X) + c))

    def send_seq(k):
        slot = halo_slot(x, c)
        return remote(chunk(me, k), chunk(slot, k), sy.at[k], rsem.at[slot, k], (seq_target(ahead), h))

    def forward(slot, k):
        return remote(
            chunk(slot, k), chunk(slot, k), sf.at[slot // 2, k], rsem.at[slot, k], (s, 2 * x + 1 - c)
        )

    def relay_seq(dx, k):
        xx = (x + dx) % X
        slot = halo_slot(xx, c)
        return remote(
            chunk(own_slot(xx, c), k), chunk(slot, k), s1.at[dx, k], rsem.at[slot, k],
            (seq_target(2 * xx >= half), h),
        )

    def relay_x(dx, k):
        slot = halo_slot(x, c)
        return remote(
            chunk(slot, k), chunk(slot, k), s2.at[dx, k - early], rsem.at[slot, k],
            (s, 2 * ((x + dx) % X) + c),
        )

    def arrived(slot, k):
        ref = chunk(slot, k)
        pltpu.make_async_copy(ref, ref, rsem.at[slot, k]).wait()

    RT = min(128, CH)

    def norm_rows(r):
        rows = pl.ds(pl.multiple_of(r * RT, RT), RT)
        v = tokens[rows, :].astype(F32)
        centred = v - jnp.mean(v, axis=-1, keepdims=True)
        spread = jnp.mean(centred * centred, axis=-1, keepdims=True)
        y = centred * lax.rsqrt(spread + EPSILON) * (1.0 + mod_scale[...]) + mod_shift[...]
        arr[me, rows, :] = y.astype(BF16)

    def send_first(k):
        for dx in range(1, X):
            send_x(dx, k).start()

    def send_halo(k):
        @pl.when(seq_exists(ahead))
        def _():
            send_seq(k).start()

    def norm_chunk(k):
        lax.fori_loop(0, CH // RT, lambda r, _: (norm_rows(k * (CH // RT) + r), 0)[1], 0)

    def start_chunk(n, _):
        k = (n % 2) * early + n // 2
        norm_chunk(k)

        @pl.when(n == 0)
        def _():
            peers = X
            for cond in (has_next, has_prev, cross_next, cross_prev):
                peers = peers + jnp.where(cond, one, none)
            pl.semaphore_wait(barrier, peers)

        @pl.when(n == 0)
        def _():
            send_first(0)

        @pl.when(n == 1)
        def _():
            send_halo(early)

        forward(me, k).start()
        return 0

    lax.fori_loop(0, NC, start_chunk, 0)

    WT = min(256, W)
    same = (
        lax.broadcasted_iota(jnp.int32, (WT, WT), 0) // HD
        == lax.broadcasted_iota(jnp.int32, (WT, WT), 1) // HD
    )
    averaging = jnp.where(same, F32(1.0 / HD), F32(0.0)).astype(BF16)
    averaging = jnp.concatenate([averaging, averaging], axis=0)

    def head_norm(v, gain):
        square = v * v
        high = square.astype(BF16)
        low = (square - high.astype(F32)).astype(BF16)
        parts = []
        for n in range(v.shape[1] // WT):
            cols = slice(n * WT, (n + 1) * WT)
            both = jnp.concatenate([high[:, cols], low[:, cols]], axis=1)
            mean = jnp.dot(both, averaging, preferred_element_type=F32)
            parts.append(v[:, cols] * lax.rsqrt(mean + EPSILON))
        return jnp.concatenate(parts, axis=1) * gain

    def rows_of(parts):
        return jnp.concatenate(
            [arr[slot, pl.ds(pl.multiple_of(k * CH, CH), CH), :] for slot, k in parts], axis=0
        )

    swap = lax.broadcasted_iota(jnp.int32, (W, 2 * BLK), 1) < BLK

    def make_kv(parts):
        v = rows_of(parts)
        key = head_norm(
            jnp.dot(v, wk[...], preferred_element_type=F32), k_gain[:, pl.ds(mine, W)]
        ).astype(BF16)
        val = lax.dot_general(wvt[...], v, (((1,), (1,)), ((), ())), preferred_element_type=F32)
        for n, (slot, k) in enumerate(parts):
            first = slot * NB + k * CB
            keys[pl.ds(first, CB)] = key[n * CH : (n + 1) * CH].reshape(CB, BLK, W)
            for m in range(CB // 2):
                pair = val[:, n * CH + m * 2 * BLK : n * CH + (m + 1) * 2 * BLK]
                turned = pltpu.roll(pair, BLK, 1)
                vals[first + 2 * m] = jnp.where(swap, pair, turned).astype(BF16)
                vals[first + 2 * m + 1] = jnp.where(swap, turned, pair).astype(BF16)

    def make_q(slot0, k):
        v = rows_of([(slot0, k), (slot0 + 1, k)])
        query = head_norm(
            jnp.dot(v, wq[...], preferred_element_type=F32), q_gain[:, pl.ds(mine, W)]
        ).astype(BF16)
        query = query * jnp.asarray(1.0 / math.sqrt(HD), BF16)
        for n in range(2):
            q[pl.ds(n * NB + k * CB, CB)] = query[n * CH : (n + 1) * CH].reshape(CB, BLK, W)

    spots = lax.broadcasted_iota(jnp.int32, (T, to_next.shape[1]), 0)
    for n, ref in enumerate((to_next, to_prev)):
        chosen[n] = jnp.where(spots == ref[...], F32(1.0), F32(0.0)).astype(BF16)
    for load in loads:
        load.wait()
    wdt[...] = wd[...].T

    def turn_values(n, _):
        rows = pl.ds(pl.multiple_of(n * 128, 128), 128)
        wvt[:, rows] = wv[rows, :].T
        return 0

    lax.fori_loop(0, D // 128, turn_values, 0)
    C = w_dec.shape[1]

    def turn_taps(n, _):
        rows = pl.ds(pl.multiple_of(n * C, C), C)
        conv_wt[:, rows] = wc[rows, :].T
        return 0

    lax.fori_loop(0, conv_w.shape[0] // C, turn_taps, 0)

    for k in range(1, early):
        send_first(k)
        send_halo(k + early)

    def own_step(k, _):
        arrived(own_slot(x, 1 - c), k)
        make_q(own_slot(x, 0), k)
        make_kv([(own_slot(x, 0), k), (own_slot(x, 1), k)])
        return 0

    lax.fori_loop(0, NC, own_step, 0)

    def send_next(i):
        def peer(dx, _):
            @pl.when(i <= early)
            def _():
                send_x(dx, i).wait_send()

            @pl.when(i < early - 1)
            def _():
                send_x(dx, i + early).start()

            @pl.when(i == early)
            def _():
                send_x(dx, NC - 1).start()

            return 0

        lax.fori_loop(1, X, peer, 0)

        @pl.when(jnp.logical_and(i <= early, seq_exists(ahead)))
        def _():
            send_seq((i + early) % NC).wait_send()

        @pl.when(jnp.logical_and(i < early - 1, seq_exists(ahead)))
        def _():
            send_seq(i).start()

        @pl.when(jnp.logical_and(i == early, seq_exists(ahead)))
        def _():
            send_seq(early - 1).start()

    def receive_step(i, _):
        send_next(i)
        late = jnp.logical_and(i >= NC - 1, i < NC - 1 + early)
        k1 = jnp.where(i < NC, i, NC - 1)

        def place(n):
            dx, over_seq = 1 + n // 2, n % 2 == 1
            xx = (x + dx) % X
            far = halo_exists(2 * xx >= half)
            near = jnp.where(over_seq, jnp.logical_and(dx == 1, halo_exists(ahead)), True)
            k = jnp.where(
                late,
                jnp.where(over_seq, i - NC + 1, i - NC + 1 + early),
                jnp.where(over_seq, (k1 + early) % NC, k1),
            )
            slot = jnp.where(
                late, halo_slot(xx, 0), jnp.where(over_seq, halo_slot(x, 0), own_slot(xx, 0))
            )

            used = jnp.logical_or(
                jnp.logical_and(late, far), jnp.logical_and(jnp.logical_not(late), near)
            )
            return used, slot, k

        def pass_on(n, _):
            used, slot, k = place(n)

            @pl.when(used)
            def _():
                arrived(slot + c, k)
                forward(slot + c, k).start()

            return 0

        def relay(dx, _):
            @pl.when(seq_exists(2 * ((x + dx) % X) >= half))
            def _():
                relay_seq(dx, i).start()

            @pl.when(halo_exists(ahead))
            def _():
                relay_x(dx, i + early).start()

            return 0

        def work(n, _):
            (used0, slot0, k0), (used1, slot1, k1) = place(2 * n), place(2 * n + 1)

            @pl.when(jnp.logical_and(used0, used1))
            def _():
                def core(t, _):
                    cc = (c + t) % 2

                    @pl.when(t == 1)
                    def _():
                        arrived(slot0 + cc, k0)
                        arrived(slot1 + cc, k1)

                    make_kv([(slot0 + cc, k0), (slot1 + cc, k1)])
                    return 0

                lax.fori_loop(0, 2, core, 0)

            @pl.when(jnp.logical_and(used0, jnp.logical_not(used1)))
            def _():
                arrived(slot0 + 1 - c, k0)
                make_kv([(slot0, k0), (slot0 + 1, k0)])

            return 0

        lax.fori_loop(0, 2 * (X - 1), pass_on, 0)

        @pl.when(i < early)
        def _():
            lax.fori_loop(1, X, relay, 0)

        lax.fori_loop(0, X - 1, work, 0)
        return 0

    lax.fori_loop(0, NC + early, receive_step, 0)

    G = WT // HD
    base = (s * H - half) * NB
    diagonal = jnp.where(
        lax.broadcasted_iota(jnp.int32, (G * BLK, WT), 0) // BLK
        == lax.broadcasted_iota(jnp.int32, (G * BLK, WT), 1) // HD,
        F32(1.0), F32(0.0),
    ).astype(BF16)
    low = lax.broadcasted_iota(jnp.int32, (WT, 2 * BLK), 1) < BLK
    head_of = lax.broadcasted_iota(jnp.int32, (HD, G * BLK), 1) // BLK

    def attend(core, b, dst):
        row = (2 * x + core) * NB + b
        local, penalty = [], []
        for n in range(KB):
            block = lists[n, row]
            live = lax.rem(block, NB) < active[block // NB]
            penalty.append(jnp.where(live, F32(0.0), F32(MASKED)))
            local.append(jnp.clip(block - base, 0, 2 * H * NB - 1))
        for g in range(W // WT):
            cols = slice(g * WT, (g + 1) * WT)
            spread = jnp.concatenate([q[core * NB + b, :, cols]] * G, axis=0) * diagonal
            key = jnp.concatenate([keys[l, :, cols] for l in local], axis=0)
            scores = lax.dot_general(key, spread, (((1,), (1,)), ((), ())), preferred_element_type=F32)
            scores = [scores[n * BLK : (n + 1) * BLK] for n in range(KB)]
            highest = functools.reduce(
                jnp.maximum, [jnp.max(v, axis=0, keepdims=True) + p for v, p in zip(scores, penalty)]
            )
            raised = [jnp.exp(v - (highest - p)) for v, p in zip(scores, penalty)]
            total = functools.reduce(jnp.add, [jnp.sum(v, axis=0, keepdims=True) for v in raised])
            scale = 1.0 / total
            weights = jnp.concatenate([(v * scale).astype(BF16) for v in raised], axis=0)
            value = jnp.concatenate(
                [
                    jnp.where(low, vals[local[n], cols, :], vals[local[n + 1], cols, :])
                    for n in range(0, KB, 2)
                ],
                axis=1,
            )
            mixed = jnp.dot(value, weights, preferred_element_type=F32)
            result = mixed[0:HD]
            for n in range(1, G):
                result = jnp.where(head_of == n, mixed[n * HD : (n + 1) * HD], result)
            result = result.T
            dst[pl.ds(pl.multiple_of(b * BLK, BLK), BLK), cols] = jnp.concatenate(
                [result[n * BLK : (n + 1) * BLK] for n in range(G)], axis=1
            ).astype(BF16)

    def attend_all(core, dst):
        def step(n, _):
            for m in range(8):
                attend(core, 8 * n + m, dst)
            return 0

        lax.fori_loop(0, NB // 8, step, 0)

    def o_copy():
        return remote(send_o, recv_o, o_ssem, o_rsem, (s, 2 * x + 1 - c))

    attend_all(1 - c, send_o)
    o_copy().start()
    attend_all(c, own_o)
    o_copy().wait_recv()

    own_live = active[device] * BLK
    OR = min(512, T)
    OC = min(512, D)

    def project_out(n, _):
        r, j = n // (D // OC), n % (D // OC)
        rows = pl.ds(pl.multiple_of(r * OR, OR), OR)
        cols = pl.ds(pl.multiple_of(j * OC, OC), OC)
        update = jnp.dot(own_o[rows, :], wo[pl.ds(mine, W), cols], preferred_element_type=F32) + jnp.dot(
            recv_o[rows, :], wo[pl.ds(other, W), cols], preferred_element_type=F32
        )
        live = lax.broadcasted_iota(jnp.int32, (OR, 1), 0) + r * OR < own_live
        residual = tokens[rows, cols].astype(F32) + attn_gate[:, cols] * update
        out_rows[rows, cols] = jnp.where(live, residual, 0.0).astype(BF16)
        return 0

    lax.fori_loop(0, (T // OR) * (D // OC), project_out, 0)
    out_copy = pltpu.make_async_copy(out_rows, block_out, out_sem)
    out_copy.start()
    features = lax.dot_general(
        wdt[...], out_rows[...], (((1,), (1,)), ((), ())), preferred_element_type=F32
    ).astype(BF16)
    for n in range(2):
        face[n] = jnp.dot(features, chosen[n], preferred_element_type=F32).astype(BF16)

    def face_copy(n, target):
        return remote(face.at[n], face_in.at[n], face_ssem.at[n], face_rsem.at[n], target)

    @pl.when(any_next)
    def _():
        face_copy(0, next_id).start()

    @pl.when(any_prev)
    def _():
        face_copy(1, prev_id).start()

    FACE = to_next.shape[1]
    SEG = pieces.shape[2]
    for n in range(T // SEG):
        pieces[n] = features[:, n * SEG : (n + 1) * SEG]
    for n, cond in ((0, any_prev), (1, any_next)):
        @pl.when(cond)
        def _():
            pltpu.make_async_copy(face_in.at[n], face_in.at[n], face_rsem.at[n]).wait()
            pieces[T // SEG, :, n * FACE : (n + 1) * FACE] = face_in[n]

        @pl.when(jnp.logical_not(cond))
        def _():
            pieces[T // SEG, :, n * FACE : (n + 1) * FACE] = jnp.zeros((pieces.shape[1], FACE), BF16)

    out_copy.wait()
    o_copy().wait_send()

    @pl.when(any_next)
    def _():
        face_copy(0, next_id).wait_send()

    @pl.when(any_prev)
    def _():
        face_copy(1, prev_id).wait_send()

    def drain(k, _):
        forward(me, k).wait_send()

        @pl.when(jnp.logical_and(k == early - 1, seq_exists(ahead)))
        def _():
            send_seq(k).wait_send()

        @pl.when(halo_exists(ahead))
        def _():
            forward(halo_slot(x, c), k).wait_send()

            @pl.when(k >= early)
            def _():
                for dx in range(1, X):
                    relay_x(dx, k).wait_send()

        def peer(dx, _):
            xx = (x + dx) % X
            forward(own_slot(xx, c), k).wait_send()

            @pl.when(k == NC - 1)
            def _():
                send_x(dx, k).wait_send()

            @pl.when(jnp.logical_and(k < early, seq_exists(2 * xx >= half)))
            def _():
                relay_seq(dx, k).wait_send()

            @pl.when(halo_exists(2 * xx >= half))
            def _():
                forward(halo_slot(xx, c), k).wait_send()

            return 0

        lax.fori_loop(1, X, peer, 0)
        return 0

    lax.fori_loop(0, NC, drain, 0)


def conv_kernel(block_in, pieces, table, conv_wt, active, block_out, decoded, held, gathered, taps, sem):
    fetch = pltpu.make_async_copy(block_in, held, sem.at[0])
    store = pltpu.make_async_copy(held, block_out, sem.at[1])
    fetch.start()
    weights = pltpu.make_async_copy(conv_wt, taps, sem.at[2])
    weights.start()
    N, C, SEG = pieces.shape
    TAPS, T = table.shape
    device = lax.axis_index("seq") * lax.axis_size("head") + lax.axis_index("head")
    spots = lax.broadcasted_iota(jnp.int32, (SEG, T), 0).astype(F32).astype(BF16)
    stacked = pieces[...].reshape(N * C, SEG)

    def gather(t):
        index = table[pl.ds(t, 1), :]
        segment = index // SEG
        offset = (index - segment * SEG).astype(F32).astype(BF16)
        onehot = jnp.where(spots == offset, BF16(1.0), BF16(0.0))
        found = jnp.dot(stacked, onehot, preferred_element_type=F32).astype(BF16)
        rows = jnp.zeros((C, T), BF16)
        for n in range(N):
            rows = jnp.where(segment == n, found[n * C : (n + 1) * C], rows)
        gathered[pl.ds(pl.multiple_of(t * C, C), C), :] = rows

    U = 9 if TAPS % 9 == 0 else 1

    def step(n, _):
        for m in range(U):
            gather(U * n + m)
        return 0

    lax.fori_loop(0, TAPS // U, step, 0)
    fetch.wait()
    store.start()
    own = jnp.concatenate([pieces[n] for n in range(T // SEG)], axis=1).astype(F32)
    weights.wait()
    total = own + jnp.dot(taps[...], gathered[...], preferred_element_type=F32)
    live = lax.broadcasted_iota(jnp.int32, (1, T), 1) < active[device] * BLK
    decoded[...] = jnp.where(live, total, 0.0).T.astype(BF16)
    store.wait()


def body(
    tokens, mod_shift, mod_scale, attn_gate, w_qkv, query_gain, key_gain, w_out, w_dec,
    conv_weight, block_lists, active_blocks, to_next, to_prev, conv_table,
):
    S, H = lax.axis_size("seq"), lax.axis_size("head")
    T, D = tokens.shape
    W = D // 2
    X = H // 2
    C = w_dec.shape[1]
    taps = conv_table.shape[1]
    face = to_next.shape[0]
    seg = 2 * face
    vmem = pl.BlockSpec(memory_space=pltpu.VMEM)
    smem = pl.BlockSpec(memory_space=pltpu.SMEM)
    hbm = pl.BlockSpec(memory_space=pl.ANY)
    dma = pltpu.SemaphoreType.DMA
    grant = 60 * 1024 * 1024
    rows, pieces, conv_wt = pl.pallas_call(
        functools.partial(block_kernel, S, H),
        out_shape=(
            jax.ShapeDtypeStruct((T, D), BF16),
            jax.ShapeDtypeStruct((T // seg + 1, C, seg), BF16),
            jax.ShapeDtypeStruct((C, taps * C), BF16),
        ),
        in_specs=[vmem] * 8 + [smem] * 2 + [hbm] * 4,
        out_specs=(hbm, vmem, vmem),
        scratch_shapes=[
            pltpu.VMEM((2 * H, T, D), BF16),
            pltpu.VMEM((2 * H * NB, BLK, W), BF16),
            pltpu.VMEM((2 * H * NB, W, 2 * BLK), BF16),
            pltpu.VMEM((2 * NB, BLK, W), BF16),
            pltpu.VMEM((D, W), BF16),
            pltpu.VMEM((D, W), BF16),
            pltpu.VMEM((D, W), BF16),
            pltpu.VMEM((W, D), BF16),
            pltpu.VMEM((D, D), BF16),
            pltpu.VMEM((D, C), BF16),
            pltpu.VMEM((C, D), BF16),
            pltpu.VMEM((taps * C, C), BF16),
            pltpu.VMEM((T, W), BF16),
            pltpu.VMEM((T, W), BF16),
            pltpu.VMEM((T, W), BF16),
            pltpu.VMEM((T, D), BF16),
            pltpu.VMEM((2, T, face), BF16),
            pltpu.VMEM((2, C, face), BF16),
            pltpu.VMEM((2, C, face), BF16),
            dma((6,)), dma, dma((2 * H, NC)), dma((X, NC)), dma((NC,)), dma((H, NC)),
            dma((X, NC // 2)), dma((X, NC // 2)), dma, dma, dma((2,)), dma((2,)),
        ],
        compiler_params=pltpu.CompilerParams(
            collective_id=0, has_side_effects=True, vmem_limit_bytes=grant
        ),
    )(
        tokens, mod_shift.reshape(1, D), mod_scale.reshape(1, D), query_gain.reshape(1, D),
        key_gain.reshape(1, D), attn_gate.reshape(1, D), to_next.reshape(1, face),
        to_prev.reshape(1, face), block_lists.T, active_blocks, w_qkv, w_out, w_dec,
        conv_weight,
    )
    return pl.pallas_call(
        conv_kernel,
        out_shape=(
            jax.ShapeDtypeStruct((T, D), BF16),
            jax.ShapeDtypeStruct((T, C), BF16),
        ),
        in_specs=[hbm, vmem, vmem, hbm, smem],
        out_specs=(hbm, vmem),
        scratch_shapes=[
            pltpu.VMEM((T, D), BF16), pltpu.VMEM((taps * C, T), BF16), pltpu.VMEM((C, taps * C), BF16), dma((3,)),
        ],
        compiler_params=pltpu.CompilerParams(vmem_limit_bytes=grant),
    )(rows, pieces, conv_table.T, conv_wt, active_blocks)


def solution(mesh):
    rows = P(("seq", "head"), None)
    return jax.shard_map(
        body,
        mesh=mesh,
        in_specs=(
            rows, P(), P(), P(), P(), P(), P(), P(), P(), P(),
            P("seq", None), P(), P(("seq", "head")), P(("seq", "head")), rows,
        ),
        out_specs=(rows, rows),
        check_vma=False,
    )
```

```python
import functools
import math

import jax
import jax.numpy as jnp
from jax import lax
from jax.experimental import pallas as pl
from jax.experimental.pallas import tpu as pltpu
from jax.sharding import PartitionSpec as P

HD = 64
BLK = 64
NB = 8
KB = 8
NC = 4
EPSILON = 1e-06
MASKED = -1000000000.0
MESH = pl.DeviceIdType.MESH
BF16 = jnp.bfloat16
F32 = jnp.float32


def block_kernel(
    S, H,
    tokens, mod_shift, mod_scale, q_gain, k_gain, attn_gate, to_next, to_prev, lists, active,
    w_qkv, w_out, w_dec, conv_w,
    block_out, pieces, conv_out,
    conv_wt, arr, keys, vals, q, wq, wk, wv, wvt, wo, wd, wdt, wc, own_o, send_o, recv_o, out_rows, chosen, face, face_in,
    w_sem, out_sem, rsem, sx, sy, sf, s1, s2, o_ssem, o_rsem, face_ssem, face_rsem,
):
    T, D = tokens.shape
    W = D // 2
    X = H // 2
    half = H // 2
    CH = T // NC
    CB = CH // BLK
    early = NC // 2
    s = lax.axis_index("seq")
    h = lax.axis_index("head")
    x, c = h // 2, h % 2
    device = s * H + h
    has_next, has_prev = s < S - 1, s > 0
    ahead = 2 * x >= half

    def seq_exists(ahead_of):
        return jnp.logical_or(
            jnp.logical_and(ahead_of, has_next), jnp.logical_and(jnp.logical_not(ahead_of), has_prev)
        )

    def halo_exists(ahead_of):
        return jnp.logical_or(
            jnp.logical_and(ahead_of, has_prev), jnp.logical_and(jnp.logical_not(ahead_of), has_next)
        )

    def seq_target(ahead_of):
        return jnp.where(ahead_of, s + 1, s - 1)

    def own_slot(xx, cc):
        return half + 2 * xx + cc

    def halo_slot(xx, cc):
        return jnp.where(2 * xx >= half, 2 * xx + cc - half, half + H + 2 * xx + cc)

    any_next, any_prev = device < S * H - 1, device > 0
    cross_next = jnp.logical_and(c == 1, any_next)
    cross_prev = jnp.logical_and(c == 0, any_prev)
    next_id = ((device + 1) // H, (device + 1) % H)
    prev_id = ((device + S * H - 1) // H % S, (device + H - 1) % H)

    one, none = jnp.int32(1), jnp.int32(0)
    barrier = pltpu.get_barrier_semaphore()
    for dx in range(1, X):
        pl.semaphore_signal(
            barrier, inc=1, device_id=(s, 2 * ((x + dx) % X) + c), device_id_type=MESH
        )
    pl.semaphore_signal(barrier, inc=1, device_id=(s, 2 * x + 1 - c), device_id_type=MESH)
    for cond, where in (
        (has_next, (s + 1, h)), (has_prev, (s - 1, h)), (cross_next, next_id), (cross_prev, prev_id)
    ):
        @pl.when(cond)
        def _():
            pl.semaphore_signal(barrier, inc=1, device_id=where, device_id_type=MESH)

    mine = pl.multiple_of(c * W, W)
    other = pl.multiple_of((1 - c) * W, W)
    loads = [
        pltpu.make_async_copy(w_qkv.at[:, pl.ds(pl.multiple_of(n * D + c * W, W), W)], ref, w_sem.at[n])
        for n, ref in enumerate((wq, wk, wv))
    ]
    loads.append(pltpu.make_async_copy(w_dec, wd, w_sem.at[3]))
    loads.append(pltpu.make_async_copy(w_out, wo, w_sem.at[4]))
    loads.append(pltpu.make_async_copy(conv_w, wc, w_sem.at[5]))
    for load in loads:
        load.start()

    def chunk(slot, k):
        return arr.at[slot, pl.ds(pl.multiple_of(k * CH, CH), CH), :]

    def remote(src, dst, ssem, recv, target):
        return pltpu.make_async_remote_copy(
            src_ref=src, dst_ref=dst, send_sem=ssem, recv_sem=recv, device_id=target, device_id_type=MESH
        )

    me = own_slot(x, c)

    def send_x(dx, k):
        return remote(chunk(me, k), chunk(me, k), sx.at[dx, k], rsem.at[me, k], (s, 2 * ((x + dx) % X) + c))

    def send_seq(k):
        slot = halo_slot(x, c)
        return remote(chunk(me, k), chunk(slot, k), sy.at[k], rsem.at[slot, k], (seq_target(ahead), h))

    def forward(slot, k):
        return remote(
            chunk(slot, k), chunk(slot, k), sf.at[slot // 2, k], rsem.at[slot, k], (s, 2 * x + 1 - c)
        )

    def relay_seq(dx, k):
        xx = (x + dx) % X
        slot = halo_slot(xx, c)
        return remote(
            chunk(own_slot(xx, c), k), chunk(slot, k), s1.at[dx, k], rsem.at[slot, k],
            (seq_target(2 * xx >= half), h),
        )

    def relay_x(dx, k):
        slot = halo_slot(x, c)
        return remote(
            chunk(slot, k), chunk(slot, k), s2.at[dx, k - early], rsem.at[slot, k],
            (s, 2 * ((x + dx) % X) + c),
        )

    def arrived(slot, k):
        ref = chunk(slot, k)
        pltpu.make_async_copy(ref, ref, rsem.at[slot, k]).wait()

    RT = min(128, CH)

    def norm_rows(r):
        rows = pl.ds(pl.multiple_of(r * RT, RT), RT)
        v = tokens[rows, :].astype(F32)
        centred = v - jnp.mean(v, axis=-1, keepdims=True)
        spread = jnp.mean(centred * centred, axis=-1, keepdims=True)
        y = centred * lax.rsqrt(spread + EPSILON) * (1.0 + mod_scale[...]) + mod_shift[...]
        arr[me, rows, :] = y.astype(BF16)

    def send_first(k):
        for dx in range(1, X):
            send_x(dx, k).start()

    def send_halo(k):
        @pl.when(seq_exists(ahead))
        def _():
            send_seq(k).start()

    def norm_chunk(k):
        lax.fori_loop(0, CH // RT, lambda r, _: (norm_rows(k * (CH // RT) + r), 0)[1], 0)

    def start_chunk(n, _):
        k = (n % 2) * early + n // 2
        norm_chunk(k)

        @pl.when(n == 0)
        def _():
            peers = X
            for cond in (has_next, has_prev, cross_next, cross_prev):
                peers = peers + jnp.where(cond, one, none)
            pl.semaphore_wait(barrier, peers)

        @pl.when(n == 0)
        def _():
            send_first(0)

        @pl.when(n == 1)
        def _():
            send_halo(early)

        forward(me, k).start()
        return 0

    lax.fori_loop(0, NC, start_chunk, 0)

    WT = min(256, W)
    same = (
        lax.broadcasted_iota(jnp.int32, (WT, WT), 0) // HD
        == lax.broadcasted_iota(jnp.int32, (WT, WT), 1) // HD
    )
    averaging = jnp.where(same, F32(1.0 / HD), F32(0.0)).astype(BF16)
    averaging = jnp.concatenate([averaging, averaging], axis=0)

    def head_norm(v, gain):
        square = v * v
        high = square.astype(BF16)
        low = (square - high.astype(F32)).astype(BF16)
        parts = []
        for n in range(v.shape[1] // WT):
            cols = slice(n * WT, (n + 1) * WT)
            both = jnp.concatenate([high[:, cols], low[:, cols]], axis=1)
            mean = jnp.dot(both, averaging, preferred_element_type=F32)
            parts.append(v[:, cols] * lax.rsqrt(mean + EPSILON))
        return jnp.concatenate(parts, axis=1) * gain

    def rows_of(parts):
        return jnp.concatenate(
            [arr[slot, pl.ds(pl.multiple_of(k * CH, CH), CH), :] for slot, k in parts], axis=0
        )

    swap = lax.broadcasted_iota(jnp.int32, (W, 2 * BLK), 1) < BLK

    def make_kv(parts):
        v = rows_of(parts)
        key = head_norm(
            jnp.dot(v, wk[...], preferred_element_type=F32), k_gain[:, pl.ds(mine, W)]
        ).astype(BF16)
        val = lax.dot_general(wvt[...], v, (((1,), (1,)), ((), ())), preferred_element_type=F32)
        for n, (slot, k) in enumerate(parts):
            first = slot * NB + k * CB
            keys[pl.ds(first, CB)] = key[n * CH : (n + 1) * CH].reshape(CB, BLK, W)
            for m in range(CB // 2):
                pair = val[:, n * CH + m * 2 * BLK : n * CH + (m + 1) * 2 * BLK]
                turned = pltpu.roll(pair, BLK, 1)
                vals[first + 2 * m] = jnp.where(swap, pair, turned).astype(BF16)
                vals[first + 2 * m + 1] = jnp.where(swap, turned, pair).astype(BF16)

    def make_q(slot0, k):
        v = rows_of([(slot0, k), (slot0 + 1, k)])
        query = head_norm(
            jnp.dot(v, wq[...], preferred_element_type=F32), q_gain[:, pl.ds(mine, W)]
        ).astype(BF16)
        query = query * jnp.asarray(1.0 / math.sqrt(HD), BF16)
        for n in range(2):
            q[pl.ds(n * NB + k * CB, CB)] = query[n * CH : (n + 1) * CH].reshape(CB, BLK, W)

    spots = lax.broadcasted_iota(jnp.int32, (T, to_next.shape[1]), 0)
    for n, ref in enumerate((to_next, to_prev)):
        chosen[n] = jnp.where(spots == ref[...], F32(1.0), F32(0.0)).astype(BF16)
    for load in loads:
        load.wait()
    wdt[...] = wd[...].T

    def turn_values(n, _):
        rows = pl.ds(pl.multiple_of(n * 128, 128), 128)
        wvt[:, rows] = wv[rows, :].T
        return 0

    lax.fori_loop(0, D // 128, turn_values, 0)
    C = w_dec.shape[1]

    def turn_taps(n, _):
        rows = pl.ds(pl.multiple_of(n * C, C), C)
        conv_wt[:, rows] = wc[rows, :].T
        return 0

    lax.fori_loop(0, conv_w.shape[0] // C, turn_taps, 0)
    taps_copy = pltpu.make_async_copy(conv_wt, conv_out, w_sem.at[6])
    taps_copy.start()

    for k in range(1, early):
        send_first(k)
        send_halo(k + early)

    def own_step(k, _):
        arrived(own_slot(x, 1 - c), k)
        make_q(own_slot(x, 0), k)
        make_kv([(own_slot(x, 0), k), (own_slot(x, 1), k)])
        return 0

    lax.fori_loop(0, NC, own_step, 0)

    def send_next(i):
        def peer(dx, _):
            @pl.when(i <= early)
            def _():
                send_x(dx, i).wait_send()

            @pl.when(i < early - 1)
            def _():
                send_x(dx, i + early).start()

            @pl.when(i == early)
            def _():
                send_x(dx, NC - 1).start()

            return 0

        lax.fori_loop(1, X, peer, 0)

        @pl.when(jnp.logical_and(i <= early, seq_exists(ahead)))
        def _():
            send_seq((i + early) % NC).wait_send()

        @pl.when(jnp.logical_and(i < early - 1, seq_exists(ahead)))
        def _():
            send_seq(i).start()

        @pl.when(jnp.logical_and(i == early, seq_exists(ahead)))
        def _():
            send_seq(early - 1).start()

    def receive_step(i, _):
        send_next(i)
        late = jnp.logical_and(i >= NC - 1, i < NC - 1 + early)
        k1 = jnp.where(i < NC, i, NC - 1)

        def place(n):
            dx, over_seq = 1 + n // 2, n % 2 == 1
            xx = (x + dx) % X
            far = halo_exists(2 * xx >= half)
            near = jnp.where(over_seq, jnp.logical_and(dx == 1, halo_exists(ahead)), True)
            k = jnp.where(
                late,
                jnp.where(over_seq, i - NC + 1, i - NC + 1 + early),
                jnp.where(over_seq, (k1 + early) % NC, k1),
            )
            slot = jnp.where(
                late, halo_slot(xx, 0), jnp.where(over_seq, halo_slot(x, 0), own_slot(xx, 0))
            )

            used = jnp.logical_or(
                jnp.logical_and(late, far), jnp.logical_and(jnp.logical_not(late), near)
            )
            return used, slot, k

        def pass_on(n, _):
            used, slot, k = place(n)

            @pl.when(used)
            def _():
                arrived(slot + c, k)
                forward(slot + c, k).start()

            return 0

        def relay(dx, _):
            @pl.when(seq_exists(2 * ((x + dx) % X) >= half))
            def _():
                relay_seq(dx, i).start()

            @pl.when(halo_exists(ahead))
            def _():
                relay_x(dx, i + early).start()

            return 0

        def work(n, _):
            (used0, slot0, k0), (used1, slot1, k1) = place(2 * n), place(2 * n + 1)

            @pl.when(jnp.logical_and(used0, used1))
            def _():
                def core(t, _):
                    cc = (c + t) % 2

                    @pl.when(t == 1)
                    def _():
                        arrived(slot0 + cc, k0)
                        arrived(slot1 + cc, k1)

                    make_kv([(slot0 + cc, k0), (slot1 + cc, k1)])
                    return 0

                lax.fori_loop(0, 2, core, 0)

            @pl.when(jnp.logical_and(used0, jnp.logical_not(used1)))
            def _():
                arrived(slot0 + 1 - c, k0)
                make_kv([(slot0, k0), (slot0 + 1, k0)])

            return 0

        lax.fori_loop(0, 2 * (X - 1), pass_on, 0)

        @pl.when(i < early)
        def _():
            lax.fori_loop(1, X, relay, 0)

        lax.fori_loop(0, X - 1, work, 0)
        return 0

    lax.fori_loop(0, NC + early, receive_step, 0)

    G = WT // HD
    base = (s * H - half) * NB
    diagonal = jnp.where(
        lax.broadcasted_iota(jnp.int32, (G * BLK, WT), 0) // BLK
        == lax.broadcasted_iota(jnp.int32, (G * BLK, WT), 1) // HD,
        F32(1.0), F32(0.0),
    ).astype(BF16)
    low = lax.broadcasted_iota(jnp.int32, (WT, 2 * BLK), 1) < BLK
    head_of = lax.broadcasted_iota(jnp.int32, (HD, G * BLK), 1) // BLK

    def attend(core, b, dst):
        row = (2 * x + core) * NB + b
        local, penalty = [], []
        for n in range(KB):
            block = lists[n, row]
            live = lax.rem(block, NB) < active[block // NB]
            penalty.append(jnp.where(live, F32(0.0), F32(MASKED)))
            local.append(jnp.clip(block - base, 0, 2 * H * NB - 1))
        for g in range(W // WT):
            cols = slice(g * WT, (g + 1) * WT)
            spread = jnp.concatenate([q[core * NB + b, :, cols]] * G, axis=0) * diagonal
            key = jnp.concatenate([keys[l, :, cols] for l in local], axis=0)
            scores = lax.dot_general(key, spread, (((1,), (1,)), ((), ())), preferred_element_type=F32)
            scores = [scores[n * BLK : (n + 1) * BLK] for n in range(KB)]
            highest = functools.reduce(
                jnp.maximum, [jnp.max(v, axis=0, keepdims=True) + p for v, p in zip(scores, penalty)]
            )
            raised = [jnp.exp(v - (highest - p)) for v, p in zip(scores, penalty)]
            total = functools.reduce(jnp.add, [jnp.sum(v, axis=0, keepdims=True) for v in raised])
            scale = 1.0 / total
            weights = jnp.concatenate([(v * scale).astype(BF16) for v in raised], axis=0)
            value = jnp.concatenate(
                [
                    jnp.where(low, vals[local[n], cols, :], vals[local[n + 1], cols, :])
                    for n in range(0, KB, 2)
                ],
                axis=1,
            )
            mixed = jnp.dot(value, weights, preferred_element_type=F32)
            result = mixed[0:HD]
            for n in range(1, G):
                result = jnp.where(head_of == n, mixed[n * HD : (n + 1) * HD], result)
            result = result.T
            dst[pl.ds(pl.multiple_of(b * BLK, BLK), BLK), cols] = jnp.concatenate(
                [result[n * BLK : (n + 1) * BLK] for n in range(G)], axis=1
            ).astype(BF16)

    def attend_all(core, dst):
        def step(n, _):
            for m in range(8):
                attend(core, 8 * n + m, dst)
            return 0

        lax.fori_loop(0, NB // 8, step, 0)

    def o_copy():
        return remote(send_o, recv_o, o_ssem, o_rsem, (s, 2 * x + 1 - c))

    attend_all(1 - c, send_o)
    o_copy().start()
    attend_all(c, own_o)
    o_copy().wait_recv()

    own_live = active[device] * BLK
    OR = min(512, T)
    OC = min(512, D)

    def project_out(n, _):
        r, j = n // (D // OC), n % (D // OC)
        rows = pl.ds(pl.multiple_of(r * OR, OR), OR)
        cols = pl.ds(pl.multiple_of(j * OC, OC), OC)
        update = jnp.dot(own_o[rows, :], wo[pl.ds(mine, W), cols], preferred_element_type=F32) + jnp.dot(
            recv_o[rows, :], wo[pl.ds(other, W), cols], preferred_element_type=F32
        )
        live = lax.broadcasted_iota(jnp.int32, (OR, 1), 0) + r * OR < own_live
        residual = tokens[rows, cols].astype(F32) + attn_gate[:, cols] * update
        out_rows[rows, cols] = jnp.where(live, residual, 0.0).astype(BF16)
        return 0

    lax.fori_loop(0, (T // OR) * (D // OC), project_out, 0)
    out_copy = pltpu.make_async_copy(out_rows, block_out, out_sem)
    out_copy.start()
    features = lax.dot_general(
        wdt[...], out_rows[...], (((1,), (1,)), ((), ())), preferred_element_type=F32
    ).astype(BF16)
    for n in range(2):
        face[n] = jnp.dot(features, chosen[n], preferred_element_type=F32).astype(BF16)

    def face_copy(n, target):
        return remote(face.at[n], face_in.at[n], face_ssem.at[n], face_rsem.at[n], target)

    @pl.when(any_next)
    def _():
        face_copy(0, next_id).start()

    @pl.when(any_prev)
    def _():
        face_copy(1, prev_id).start()

    FACE = to_next.shape[1]
    SEG = pieces.shape[2]
    for n in range(T // SEG):
        pieces[n] = features[:, n * SEG : (n + 1) * SEG]
    def drain(k, _):
        forward(me, k).wait_send()

        @pl.when(jnp.logical_and(k == early - 1, seq_exists(ahead)))
        def _():
            send_seq(k).wait_send()

        @pl.when(halo_exists(ahead))
        def _():
            forward(halo_slot(x, c), k).wait_send()

            @pl.when(k >= early)
            def _():
                for dx in range(1, X):
                    relay_x(dx, k).wait_send()

        def peer(dx, _):
            xx = (x + dx) % X
            forward(own_slot(xx, c), k).wait_send()

            @pl.when(k == NC - 1)
            def _():
                send_x(dx, k).wait_send()

            @pl.when(jnp.logical_and(k < early, seq_exists(2 * xx >= half)))
            def _():
                relay_seq(dx, k).wait_send()

            @pl.when(halo_exists(2 * xx >= half))
            def _():
                forward(halo_slot(xx, c), k).wait_send()

            return 0

        lax.fori_loop(1, X, peer, 0)
        return 0

    lax.fori_loop(0, NC, drain, 0)
    out_copy.wait()
    taps_copy.wait()
    o_copy().wait_send()
    for n, cond in ((0, any_prev), (1, any_next)):
        @pl.when(cond)
        def _():
            pltpu.make_async_copy(face_in.at[n], face_in.at[n], face_rsem.at[n]).wait()
            pieces[T // SEG, :, n * FACE : (n + 1) * FACE] = face_in[n]

        @pl.when(jnp.logical_not(cond))
        def _():
            pieces[T // SEG, :, n * FACE : (n + 1) * FACE] = jnp.zeros((pieces.shape[1], FACE), BF16)

    @pl.when(any_next)
    def _():
        face_copy(0, next_id).wait_send()

    @pl.when(any_prev)
    def _():
        face_copy(1, prev_id).wait_send()


def conv_kernel(block_in, pieces, table, conv_wt, active, block_out, decoded, held, gathered, taps, sem):
    fetch = pltpu.make_async_copy(block_in, held, sem.at[0])
    store = pltpu.make_async_copy(held, block_out, sem.at[1])
    fetch.start()
    weights = pltpu.make_async_copy(conv_wt, taps, sem.at[2])
    weights.start()
    N, C, SEG = pieces.shape
    TAPS, T = table.shape
    device = lax.axis_index("seq") * lax.axis_size("head") + lax.axis_index("head")
    spots = lax.broadcasted_iota(jnp.int32, (SEG, T), 0).astype(F32).astype(BF16)
    stacked = pieces[...].reshape(N * C, SEG)

    def gather(t):
        index = table[pl.ds(t, 1), :]
        segment = index // SEG
        offset = (index - segment * SEG).astype(F32).astype(BF16)
        onehot = jnp.where(spots == offset, BF16(1.0), BF16(0.0))
        found = jnp.dot(stacked, onehot, preferred_element_type=F32).astype(BF16)
        rows = jnp.zeros((C, T), BF16)
        for n in range(N):
            rows = jnp.where(segment == n, found[n * C : (n + 1) * C], rows)
        gathered[pl.ds(pl.multiple_of(t * C, C), C), :] = rows

    U = TAPS

    def step(n, _):
        for m in range(U):
            gather(U * n + m)
        return 0

    lax.fori_loop(0, TAPS // U, step, 0)
    fetch.wait()
    store.start()
    own = jnp.concatenate([pieces[n] for n in range(T // SEG)], axis=1).astype(F32)
    weights.wait()
    total = own + jnp.dot(taps[...], gathered[...], preferred_element_type=F32)
    live = lax.broadcasted_iota(jnp.int32, (1, T), 1) < active[device] * BLK
    decoded[...] = jnp.where(live, total, 0.0).T.astype(BF16)
    store.wait()


def body(
    tokens, mod_shift, mod_scale, attn_gate, w_qkv, query_gain, key_gain, w_out, w_dec,
    conv_weight, block_lists, active_blocks, to_next, to_prev, conv_table,
):
    S, H = lax.axis_size("seq"), lax.axis_size("head")
    T, D = tokens.shape
    W = D // 2
    X = H // 2
    C = w_dec.shape[1]
    taps = conv_table.shape[1]
    face = to_next.shape[0]
    seg = 2 * face
    vmem = pl.BlockSpec(memory_space=pltpu.VMEM)
    smem = pl.BlockSpec(memory_space=pltpu.SMEM)
    hbm = pl.BlockSpec(memory_space=pl.ANY)
    dma = pltpu.SemaphoreType.DMA
    grant = 60 * 1024 * 1024
    rows, pieces, conv_wt = pl.pallas_call(
        functools.partial(block_kernel, S, H),
        out_shape=(
            jax.ShapeDtypeStruct((T, D), BF16),
            jax.ShapeDtypeStruct((T // seg + 1, C, seg), BF16),
            jax.ShapeDtypeStruct((C, taps * C), BF16),
        ),
        in_specs=[vmem] * 8 + [smem] * 2 + [hbm] * 4,
        out_specs=(hbm, vmem, hbm),
        scratch_shapes=[
            pltpu.VMEM((C, taps * C), BF16),
            pltpu.VMEM((2 * H, T, D), BF16),
            pltpu.VMEM((2 * H * NB, BLK, W), BF16),
            pltpu.VMEM((2 * H * NB, W, 2 * BLK), BF16),
            pltpu.VMEM((2 * NB, BLK, W), BF16),
            pltpu.VMEM((D, W), BF16),
            pltpu.VMEM((D, W), BF16),
            pltpu.VMEM((D, W), BF16),
            pltpu.VMEM((W, D), BF16),
            pltpu.VMEM((D, D), BF16),
            pltpu.VMEM((D, C), BF16),
            pltpu.VMEM((C, D), BF16),
            pltpu.VMEM((taps * C, C), BF16),
            pltpu.VMEM((T, W), BF16),
            pltpu.VMEM((T, W), BF16),
            pltpu.VMEM((T, W), BF16),
            pltpu.VMEM((T, D), BF16),
            pltpu.VMEM((2, T, face), BF16),
            pltpu.VMEM((2, C, face), BF16),
            pltpu.VMEM((2, C, face), BF16),
            dma((7,)), dma, dma((2 * H, NC)), dma((X, NC)), dma((NC,)), dma((H, NC)),
            dma((X, NC // 2)), dma((X, NC // 2)), dma, dma, dma((2,)), dma((2,)),
        ],
        compiler_params=pltpu.CompilerParams(
            collective_id=0, has_side_effects=True, vmem_limit_bytes=grant
        ),
    )(
        tokens, mod_shift.reshape(1, D), mod_scale.reshape(1, D), query_gain.reshape(1, D),
        key_gain.reshape(1, D), attn_gate.reshape(1, D), to_next.reshape(1, face),
        to_prev.reshape(1, face), block_lists.T, active_blocks, w_qkv, w_out, w_dec,
        conv_weight,
    )
    return pl.pallas_call(
        conv_kernel,
        out_shape=(
            jax.ShapeDtypeStruct((T, D), BF16),
            jax.ShapeDtypeStruct((T, C), BF16),
        ),
        in_specs=[hbm, vmem, vmem, hbm, smem],
        out_specs=(hbm, vmem),
        scratch_shapes=[
            pltpu.VMEM((T, D), BF16), pltpu.VMEM((taps * C, T), BF16), pltpu.VMEM((C, taps * C), BF16), dma((3,)),
        ],
        compiler_params=pltpu.CompilerParams(vmem_limit_bytes=grant),
    )(rows, pieces, conv_table.T, conv_wt, active_blocks)


def solution(mesh):
    rows = P(("seq", "head"), None)
    return jax.shard_map(
        body,
        mesh=mesh,
        in_specs=(
            rows, P(), P(), P(), P(), P(), P(), P(), P(), P(),
            P("seq", None), P(), P(("seq", "head")), P(("seq", "head")), rows,
        ),
        out_specs=(rows, rows),
        check_vma=False,
    )
```

```python
import functools
import math

import jax
import jax.numpy as jnp
from jax import lax
from jax.experimental import pallas as pl
from jax.experimental.pallas import tpu as pltpu
from jax.sharding import PartitionSpec as P

HD = 64
BLK = 64
NB = 8
KB = 8
NC = 4
EPSILON = 1e-06
MASKED = -1000000000.0
MESH = pl.DeviceIdType.MESH
BF16 = jnp.bfloat16
F32 = jnp.float32


def block_kernel(
    S, H,
    tokens, mod_shift, mod_scale, q_gain, k_gain, attn_gate, to_next, to_prev, lists, active,
    w_qkv, w_out, w_dec, conv_w,
    block_out, pieces, conv_out,
    conv_wt, arr, keys, vals, q, wq, wk, wv, wvt, wo, wd, wdt, wc, own_o, send_o, recv_o, out_rows, chosen, face, face_in,
    w_sem, out_sem, rsem, sx, sy, sf, s1, s2, o_ssem, o_rsem, face_ssem, face_rsem,
):
    T, D = tokens.shape
    W = D // 2
    X = H // 2
    half = H // 2
    CH = T // NC
    CB = CH // BLK
    early = NC // 2
    s = lax.axis_index("seq")
    h = lax.axis_index("head")
    x, c = h // 2, h % 2
    device = s * H + h
    has_next, has_prev = s < S - 1, s > 0
    ahead = 2 * x >= half

    def seq_exists(ahead_of):
        return jnp.logical_or(
            jnp.logical_and(ahead_of, has_next), jnp.logical_and(jnp.logical_not(ahead_of), has_prev)
        )

    def halo_exists(ahead_of):
        return jnp.logical_or(
            jnp.logical_and(ahead_of, has_prev), jnp.logical_and(jnp.logical_not(ahead_of), has_next)
        )

    def seq_target(ahead_of):
        return jnp.where(ahead_of, s + 1, s - 1)

    def own_slot(xx, cc):
        return half + 2 * xx + cc

    def halo_slot(xx, cc):
        return jnp.where(2 * xx >= half, 2 * xx + cc - half, half + H + 2 * xx + cc)

    any_next, any_prev = device < S * H - 1, device > 0
    cross_next = jnp.logical_and(c == 1, any_next)
    cross_prev = jnp.logical_and(c == 0, any_prev)
    next_id = ((device + 1) // H, (device + 1) % H)
    prev_id = ((device + S * H - 1) // H % S, (device + H - 1) % H)

    one, none = jnp.int32(1), jnp.int32(0)
    barrier = pltpu.get_barrier_semaphore()
    for dx in range(1, X):
        pl.semaphore_signal(
            barrier, inc=1, device_id=(s, 2 * ((x + dx) % X) + c), device_id_type=MESH
        )
    pl.semaphore_signal(barrier, inc=1, device_id=(s, 2 * x + 1 - c), device_id_type=MESH)
    for cond, where in (
        (has_next, (s + 1, h)), (has_prev, (s - 1, h)), (cross_next, next_id), (cross_prev, prev_id)
    ):
        @pl.when(cond)
        def _():
            pl.semaphore_signal(barrier, inc=1, device_id=where, device_id_type=MESH)

    mine = pl.multiple_of(c * W, W)
    other = pl.multiple_of((1 - c) * W, W)
    loads = [
        pltpu.make_async_copy(w_qkv.at[:, pl.ds(pl.multiple_of(n * D + c * W, W), W)], ref, w_sem.at[n])
        for n, ref in enumerate((wq, wk, wv))
    ]
    loads.append(pltpu.make_async_copy(w_dec, wd, w_sem.at[3]))
    loads.append(pltpu.make_async_copy(w_out, wo, w_sem.at[4]))
    loads.append(pltpu.make_async_copy(conv_w, wc, w_sem.at[5]))
    for load in loads:
        load.start()

    def chunk(slot, k):
        return arr.at[slot, pl.ds(pl.multiple_of(k * CH, CH), CH), :]

    def remote(src, dst, ssem, recv, target):
        return pltpu.make_async_remote_copy(
            src_ref=src, dst_ref=dst, send_sem=ssem, recv_sem=recv, device_id=target, device_id_type=MESH
        )

    me = own_slot(x, c)

    def send_x(dx, k):
        return remote(chunk(me, k), chunk(me, k), sx.at[dx, k], rsem.at[me, k], (s, 2 * ((x + dx) % X) + c))

    def send_seq(k):
        slot = halo_slot(x, c)
        return remote(chunk(me, k), chunk(slot, k), sy.at[k], rsem.at[slot, k], (seq_target(ahead), h))

    def forward(slot, k):
        return remote(
            chunk(slot, k), chunk(slot, k), sf.at[slot // 2, k], rsem.at[slot, k], (s, 2 * x + 1 - c)
        )

    def relay_seq(dx, k):
        xx = (x + dx) % X
        slot = halo_slot(xx, c)
        return remote(
            chunk(own_slot(xx, c), k), chunk(slot, k), s1.at[dx, k], rsem.at[slot, k],
            (seq_target(2 * xx >= half), h),
        )

    def relay_x(dx, k):
        slot = halo_slot(x, c)
        return remote(
            chunk(slot, k), chunk(slot, k), s2.at[dx, k - early], rsem.at[slot, k],
            (s, 2 * ((x + dx) % X) + c),
        )

    def arrived(slot, k):
        ref = chunk(slot, k)
        pltpu.make_async_copy(ref, ref, rsem.at[slot, k]).wait()

    RT = min(128, CH)

    def norm_rows(r):
        rows = pl.ds(pl.multiple_of(r * RT, RT), RT)
        v = tokens[rows, :].astype(F32)
        centred = v - jnp.mean(v, axis=-1, keepdims=True)
        spread = jnp.mean(centred * centred, axis=-1, keepdims=True)
        y = centred * lax.rsqrt(spread + EPSILON) * (1.0 + mod_scale[...]) + mod_shift[...]
        arr[me, rows, :] = y.astype(BF16)

    def send_first(k):
        for dx in range(1, X):
            send_x(dx, k).start()

    def send_halo(k):
        @pl.when(seq_exists(ahead))
        def _():
            send_seq(k).start()

    def norm_chunk(k):
        lax.fori_loop(0, CH // RT, lambda r, _: (norm_rows(k * (CH // RT) + r), 0)[1], 0)

    def start_chunk(n, _):
        k = (n % 2) * early + n // 2
        norm_chunk(k)

        @pl.when(n == 0)
        def _():
            peers = X
            for cond in (has_next, has_prev, cross_next, cross_prev):
                peers = peers + jnp.where(cond, one, none)
            pl.semaphore_wait(barrier, peers)

        @pl.when(n == 0)
        def _():
            send_first(0)

        @pl.when(n == 1)
        def _():
            send_halo(early)

        forward(me, k).start()
        return 0

    lax.fori_loop(0, NC, start_chunk, 0)

    WT = min(256, W)
    same = (
        lax.broadcasted_iota(jnp.int32, (WT, WT), 0) // HD
        == lax.broadcasted_iota(jnp.int32, (WT, WT), 1) // HD
    )
    averaging = jnp.where(same, F32(1.0 / HD), F32(0.0)).astype(BF16)
    averaging = jnp.concatenate([averaging, averaging], axis=0)

    def head_norm(v, gain):
        square = v * v
        high = square.astype(BF16)
        low = (square - high.astype(F32)).astype(BF16)
        parts = []
        for n in range(v.shape[1] // WT):
            cols = slice(n * WT, (n + 1) * WT)
            both = jnp.concatenate([high[:, cols], low[:, cols]], axis=1)
            mean = jnp.dot(both, averaging, preferred_element_type=F32)
            parts.append(v[:, cols] * lax.rsqrt(mean + EPSILON))
        return jnp.concatenate(parts, axis=1) * gain

    def rows_of(parts):
        return jnp.concatenate(
            [arr[slot, pl.ds(pl.multiple_of(k * CH, CH), CH), :] for slot, k in parts], axis=0
        )

    swap = lax.broadcasted_iota(jnp.int32, (W, 2 * BLK), 1) < BLK

    def make_kv(parts):
        v = rows_of(parts)
        key = head_norm(
            jnp.dot(v, wk[...], preferred_element_type=F32), k_gain[:, pl.ds(mine, W)]
        ).astype(BF16)
        val = lax.dot_general(wvt[...], v, (((1,), (1,)), ((), ())), preferred_element_type=F32)
        for n, (slot, k) in enumerate(parts):
            first = slot * NB + k * CB
            keys[pl.ds(first, CB)] = key[n * CH : (n + 1) * CH].reshape(CB, BLK, W)
            for m in range(CB // 2):
                pair = val[:, n * CH + m * 2 * BLK : n * CH + (m + 1) * 2 * BLK]
                turned = pltpu.roll(pair, BLK, 1)
                vals[first + 2 * m] = jnp.where(swap, pair, turned).astype(BF16)
                vals[first + 2 * m + 1] = jnp.where(swap, turned, pair).astype(BF16)

    def make_q(slot0, k):
        v = rows_of([(slot0, k), (slot0 + 1, k)])
        query = head_norm(
            jnp.dot(v, wq[...], preferred_element_type=F32), q_gain[:, pl.ds(mine, W)]
        ).astype(BF16)
        query = query * jnp.asarray(1.0 / math.sqrt(HD), BF16)
        for n in range(2):
            q[pl.ds(n * NB + k * CB, CB)] = query[n * CH : (n + 1) * CH].reshape(CB, BLK, W)

    spots = lax.broadcasted_iota(jnp.int32, (T, to_next.shape[1]), 0)
    for n, ref in enumerate((to_next, to_prev)):
        chosen[n] = jnp.where(spots == ref[...], F32(1.0), F32(0.0)).astype(BF16)
    for load in loads:
        load.wait()
    wdt[...] = wd[...].T

    def turn_values(n, _):
        rows = pl.ds(pl.multiple_of(n * 128, 128), 128)
        wvt[:, rows] = wv[rows, :].T
        return 0

    lax.fori_loop(0, D // 128, turn_values, 0)
    C = w_dec.shape[1]

    def turn_taps(n, _):
        rows = pl.ds(pl.multiple_of(n * C, C), C)
        conv_wt[:, rows] = wc[rows, :].T
        return 0

    lax.fori_loop(0, conv_w.shape[0] // C, turn_taps, 0)
    taps_copy = pltpu.make_async_copy(conv_wt, conv_out, w_sem.at[6])
    taps_copy.start()

    for k in range(1, early):
        send_first(k)
        send_halo(k + early)

    def own_step(k, _):
        arrived(own_slot(x, 1 - c), k)
        make_q(own_slot(x, 0), k)
        make_kv([(own_slot(x, 0), k), (own_slot(x, 1), k)])
        return 0

    lax.fori_loop(0, NC, own_step, 0)

    def send_next(i):
        def peer(dx, _):
            @pl.when(i <= early)
            def _():
                send_x(dx, i).wait_send()

            @pl.when(i < early - 1)
            def _():
                send_x(dx, i + early).start()

            @pl.when(i == early)
            def _():
                send_x(dx, NC - 1).start()

            return 0

        lax.fori_loop(1, X, peer, 0)

        @pl.when(jnp.logical_and(i <= early, seq_exists(ahead)))
        def _():
            send_seq((i + early) % NC).wait_send()

        @pl.when(jnp.logical_and(i < early - 1, seq_exists(ahead)))
        def _():
            send_seq(i).start()

        @pl.when(jnp.logical_and(i == early, seq_exists(ahead)))
        def _():
            send_seq(early - 1).start()

    def receive_step(i, _):
        send_next(i)
        late = jnp.logical_and(i >= NC - 1, i < NC - 1 + early)
        k1 = jnp.where(i < NC, i, NC - 1)

        def place(n):
            dx, over_seq = 1 + n // 2, n % 2 == 1
            xx = (x + dx) % X
            far = halo_exists(2 * xx >= half)
            near = jnp.where(over_seq, jnp.logical_and(dx == 1, halo_exists(ahead)), True)
            k = jnp.where(
                late,
                jnp.where(over_seq, i - NC + 1, i - NC + 1 + early),
                jnp.where(over_seq, (k1 + early) % NC, k1),
            )
            slot = jnp.where(
                late, halo_slot(xx, 0), jnp.where(over_seq, halo_slot(x, 0), own_slot(xx, 0))
            )

            used = jnp.logical_or(
                jnp.logical_and(late, far), jnp.logical_and(jnp.logical_not(late), near)
            )
            return used, slot, k

        def pass_on(n, _):
            used, slot, k = place(n)

            @pl.when(used)
            def _():
                arrived(slot + c, k)
                forward(slot + c, k).start()

            return 0

        def relay(dx, _):
            @pl.when(seq_exists(2 * ((x + dx) % X) >= half))
            def _():
                relay_seq(dx, i).start()

            @pl.when(halo_exists(ahead))
            def _():
                relay_x(dx, i + early).start()

            return 0

        def work(n, _):
            (used0, slot0, k0), (used1, slot1, k1) = place(2 * n), place(2 * n + 1)

            @pl.when(jnp.logical_and(used0, used1))
            def _():
                def core(t, _):
                    cc = (c + t) % 2

                    @pl.when(t == 1)
                    def _():
                        arrived(slot0 + cc, k0)
                        arrived(slot1 + cc, k1)

                    make_kv([(slot0 + cc, k0), (slot1 + cc, k1)])
                    return 0

                lax.fori_loop(0, 2, core, 0)

            @pl.when(jnp.logical_and(used0, jnp.logical_not(used1)))
            def _():
                arrived(slot0 + 1 - c, k0)
                make_kv([(slot0, k0), (slot0 + 1, k0)])

            return 0

        lax.fori_loop(0, 2 * (X - 1), pass_on, 0)

        @pl.when(i < early)
        def _():
            lax.fori_loop(1, X, relay, 0)

        lax.fori_loop(0, X - 1, work, 0)
        return 0

    lax.fori_loop(0, NC + early, receive_step, 0)

    G = WT // HD
    base = (s * H - half) * NB
    diagonal = jnp.where(
        lax.broadcasted_iota(jnp.int32, (G * BLK, WT), 0) // BLK
        == lax.broadcasted_iota(jnp.int32, (G * BLK, WT), 1) // HD,
        F32(1.0), F32(0.0),
    ).astype(BF16)
    low = lax.broadcasted_iota(jnp.int32, (WT, 2 * BLK), 1) < BLK
    head_of = lax.broadcasted_iota(jnp.int32, (HD, G * BLK), 1) // BLK

    def attend(core, b, dst):
        row = (2 * x + core) * NB + b
        local, penalty = [], []
        for n in range(KB):
            block = lists[n, row]
            live = lax.rem(block, NB) < active[block // NB]
            penalty.append(jnp.where(live, F32(0.0), F32(MASKED)))
            local.append(jnp.clip(block - base, 0, 2 * H * NB - 1))
        for g in range(W // WT):
            cols = slice(g * WT, (g + 1) * WT)
            spread = jnp.concatenate([q[core * NB + b, :, cols]] * G, axis=0) * diagonal
            key = jnp.concatenate([keys[l, :, cols] for l in local], axis=0)
            scores = lax.dot_general(key, spread, (((1,), (1,)), ((), ())), preferred_element_type=F32)
            scores = [scores[n * BLK : (n + 1) * BLK] for n in range(KB)]
            highest = functools.reduce(
                jnp.maximum, [jnp.max(v, axis=0, keepdims=True) + p for v, p in zip(scores, penalty)]
            )
            raised = [jnp.exp(v - (highest - p)) for v, p in zip(scores, penalty)]
            total = functools.reduce(jnp.add, [jnp.sum(v, axis=0, keepdims=True) for v in raised])
            scale = 1.0 / total
            weights = jnp.concatenate([(v * scale).astype(BF16) for v in raised], axis=0)
            value = jnp.concatenate(
                [
                    jnp.where(low, vals[local[n], cols, :], vals[local[n + 1], cols, :])
                    for n in range(0, KB, 2)
                ],
                axis=1,
            )
            mixed = jnp.dot(value, weights, preferred_element_type=F32)
            result = mixed[0:HD]
            for n in range(1, G):
                result = jnp.where(head_of == n, mixed[n * HD : (n + 1) * HD], result)
            result = result.T
            dst[pl.ds(pl.multiple_of(b * BLK, BLK), BLK), cols] = jnp.concatenate(
                [result[n * BLK : (n + 1) * BLK] for n in range(G)], axis=1
            ).astype(BF16)

    def attend_all(core, dst):
        def step(n, _):
            for m in range(8):
                attend(core, 8 * n + m, dst)
            return 0

        lax.fori_loop(0, NB // 8, step, 0)

    def o_copy():
        return remote(send_o, recv_o, o_ssem, o_rsem, (s, 2 * x + 1 - c))

    attend_all(1 - c, send_o)
    o_copy().start()
    attend_all(c, own_o)
    o_copy().wait_recv()

    own_live = active[device] * BLK
    OR = min(512, T)
    OC = D

    def project_out(n, _):
        r, j = n // (D // OC), n % (D // OC)
        rows = pl.ds(pl.multiple_of(r * OR, OR), OR)
        cols = pl.ds(pl.multiple_of(j * OC, OC), OC)
        update = jnp.dot(own_o[rows, :], wo[pl.ds(mine, W), cols], preferred_element_type=F32) + jnp.dot(
            recv_o[rows, :], wo[pl.ds(other, W), cols], preferred_element_type=F32
        )
        live = lax.broadcasted_iota(jnp.int32, (OR, 1), 0) + r * OR < own_live
        residual = tokens[rows, cols].astype(F32) + attn_gate[:, cols] * update
        out_rows[rows, cols] = jnp.where(live, residual, 0.0).astype(BF16)
        return 0

    lax.fori_loop(0, (T // OR) * (D // OC), project_out, 0)
    out_copy = pltpu.make_async_copy(out_rows, block_out, out_sem)
    out_copy.start()
    features = lax.dot_general(
        wdt[...], out_rows[...], (((1,), (1,)), ((), ())), preferred_element_type=F32
    ).astype(BF16)
    for n in range(2):
        face[n] = jnp.dot(features, chosen[n], preferred_element_type=F32).astype(BF16)

    def face_copy(n, target):
        return remote(face.at[n], face_in.at[n], face_ssem.at[n], face_rsem.at[n], target)

    @pl.when(any_next)
    def _():
        face_copy(0, next_id).start()

    @pl.when(any_prev)
    def _():
        face_copy(1, prev_id).start()

    FACE = to_next.shape[1]
    SEG = pieces.shape[2]
    for n in range(T // SEG):
        pieces[n] = features[:, n * SEG : (n + 1) * SEG]
    def drain(k, _):
        forward(me, k).wait_send()

        @pl.when(jnp.logical_and(k == early - 1, seq_exists(ahead)))
        def _():
            send_seq(k).wait_send()

        @pl.when(halo_exists(ahead))
        def _():
            forward(halo_slot(x, c), k).wait_send()

            @pl.when(k >= early)
            def _():
                for dx in range(1, X):
                    relay_x(dx, k).wait_send()

        def peer(dx, _):
            xx = (x + dx) % X
            forward(own_slot(xx, c), k).wait_send()

            @pl.when(k == NC - 1)
            def _():
                send_x(dx, k).wait_send()

            @pl.when(jnp.logical_and(k < early, seq_exists(2 * xx >= half)))
            def _():
                relay_seq(dx, k).wait_send()

            @pl.when(halo_exists(2 * xx >= half))
            def _():
                forward(halo_slot(xx, c), k).wait_send()

            return 0

        lax.fori_loop(1, X, peer, 0)
        return 0

    lax.fori_loop(0, NC, drain, 0)
    out_copy.wait()
    taps_copy.wait()
    o_copy().wait_send()
    for n, cond in ((0, any_prev), (1, any_next)):
        @pl.when(cond)
        def _():
            pltpu.make_async_copy(face_in.at[n], face_in.at[n], face_rsem.at[n]).wait()
            pieces[T // SEG, :, n * FACE : (n + 1) * FACE] = face_in[n]

        @pl.when(jnp.logical_not(cond))
        def _():
            pieces[T // SEG, :, n * FACE : (n + 1) * FACE] = jnp.zeros((pieces.shape[1], FACE), BF16)

    @pl.when(any_next)
    def _():
        face_copy(0, next_id).wait_send()

    @pl.when(any_prev)
    def _():
        face_copy(1, prev_id).wait_send()


def conv_kernel(block_in, pieces, table, conv_wt, active, block_out, decoded, held, gathered, taps, sem):
    fetch = pltpu.make_async_copy(block_in, held, sem.at[0])
    store = pltpu.make_async_copy(held, block_out, sem.at[1])
    fetch.start()
    weights = pltpu.make_async_copy(conv_wt, taps, sem.at[2])
    weights.start()
    N, C, SEG = pieces.shape
    TAPS, T = table.shape
    device = lax.axis_index("seq") * lax.axis_size("head") + lax.axis_index("head")
    spots = lax.broadcasted_iota(jnp.int32, (SEG, T), 0).astype(F32).astype(BF16)
    stacked = pieces[...].reshape(N * C, SEG)

    def gather(t):
        index = table[pl.ds(t, 1), :]
        segment = index // SEG
        offset = (index - segment * SEG).astype(F32).astype(BF16)
        onehot = jnp.where(spots == offset, BF16(1.0), BF16(0.0))
        found = jnp.dot(stacked, onehot, preferred_element_type=F32).astype(BF16)
        rows = jnp.zeros((C, T), BF16)
        for n in range(N):
            rows = jnp.where(segment == n, found[n * C : (n + 1) * C], rows)
        gathered[pl.ds(pl.multiple_of(t * C, C), C), :] = rows

    U = TAPS

    def step(n, _):
        for m in range(U):
            gather(U * n + m)
        return 0

    lax.fori_loop(0, TAPS // U, step, 0)
    fetch.wait()
    store.start()
    own = jnp.concatenate([pieces[n] for n in range(T // SEG)], axis=1).astype(F32)
    weights.wait()
    total = own + jnp.dot(taps[...], gathered[...], preferred_element_type=F32)
    live = lax.broadcasted_iota(jnp.int32, (1, T), 1) < active[device] * BLK
    decoded[...] = jnp.where(live, total, 0.0).T.astype(BF16)
    store.wait()


def body(
    tokens, mod_shift, mod_scale, attn_gate, w_qkv, query_gain, key_gain, w_out, w_dec,
    conv_weight, block_lists, active_blocks, to_next, to_prev, conv_table,
):
    S, H = lax.axis_size("seq"), lax.axis_size("head")
    T, D = tokens.shape
    W = D // 2
    X = H // 2
    C = w_dec.shape[1]
    taps = conv_table.shape[1]
    face = to_next.shape[0]
    seg = 2 * face
    vmem = pl.BlockSpec(memory_space=pltpu.VMEM)
    smem = pl.BlockSpec(memory_space=pltpu.SMEM)
    hbm = pl.BlockSpec(memory_space=pl.ANY)
    dma = pltpu.SemaphoreType.DMA
    grant = 60 * 1024 * 1024
    rows, pieces, conv_wt = pl.pallas_call(
        functools.partial(block_kernel, S, H),
        out_shape=(
            jax.ShapeDtypeStruct((T, D), BF16),
            jax.ShapeDtypeStruct((T // seg + 1, C, seg), BF16),
            jax.ShapeDtypeStruct((C, taps * C), BF16),
        ),
        in_specs=[vmem] * 8 + [smem] * 2 + [hbm] * 4,
        out_specs=(hbm, vmem, hbm),
        scratch_shapes=[
            pltpu.VMEM((C, taps * C), BF16),
            pltpu.VMEM((2 * H, T, D), BF16),
            pltpu.VMEM((2 * H * NB, BLK, W), BF16),
            pltpu.VMEM((2 * H * NB, W, 2 * BLK), BF16),
            pltpu.VMEM((2 * NB, BLK, W), BF16),
            pltpu.VMEM((D, W), BF16),
            pltpu.VMEM((D, W), BF16),
            pltpu.VMEM((D, W), BF16),
            pltpu.VMEM((W, D), BF16),
            pltpu.VMEM((D, D), BF16),
            pltpu.VMEM((D, C), BF16),
            pltpu.VMEM((C, D), BF16),
            pltpu.VMEM((taps * C, C), BF16),
            pltpu.VMEM((T, W), BF16),
            pltpu.VMEM((T, W), BF16),
            pltpu.VMEM((T, W), BF16),
            pltpu.VMEM((T, D), BF16),
            pltpu.VMEM((2, T, face), BF16),
            pltpu.VMEM((2, C, face), BF16),
            pltpu.VMEM((2, C, face), BF16),
            dma((7,)), dma, dma((2 * H, NC)), dma((X, NC)), dma((NC,)), dma((H, NC)),
            dma((X, NC // 2)), dma((X, NC // 2)), dma, dma, dma((2,)), dma((2,)),
        ],
        compiler_params=pltpu.CompilerParams(
            collective_id=0, has_side_effects=True, vmem_limit_bytes=grant
        ),
    )(
        tokens, mod_shift.reshape(1, D), mod_scale.reshape(1, D), query_gain.reshape(1, D),
        key_gain.reshape(1, D), attn_gate.reshape(1, D), to_next.reshape(1, face),
        to_prev.reshape(1, face), block_lists.T, active_blocks, w_qkv, w_out, w_dec,
        conv_weight,
    )
    return pl.pallas_call(
        conv_kernel,
        out_shape=(
            jax.ShapeDtypeStruct((T, D), BF16),
            jax.ShapeDtypeStruct((T, C), BF16),
        ),
        in_specs=[hbm, vmem, vmem, hbm, smem],
        out_specs=(hbm, vmem),
        scratch_shapes=[
            pltpu.VMEM((T, D), BF16), pltpu.VMEM((taps * C, T), BF16), pltpu.VMEM((C, taps * C), BF16), dma((3,)),
        ],
        compiler_params=pltpu.CompilerParams(vmem_limit_bytes=grant),
    )(rows, pieces, conv_table.T, conv_wt, active_blocks)


def solution(mesh):
    rows = P(("seq", "head"), None)
    return jax.shard_map(
        body,
        mesh=mesh,
        in_specs=(
            rows, P(), P(), P(), P(), P(), P(), P(), P(), P(),
            P("seq", None), P(), P(("seq", "head")), P(("seq", "head")), rows,
        ),
        out_specs=(rows, rows),
        check_vma=False,
    )
```
